256 devices in a mesh: gx: 2 (over core), gy: 2 (over x_hi), gz: 64 (over z, y, x_lo).
Axes of the slice: x: 4 (x_hi: 2, x_lo: 2; x = x_hi * 2 + x_lo), y: 4, z: 8, core: 2. Of those that a mesh axis runs over, the one named last changes fastest.
Arguments:
- zvecs: bfloat16 [512, 3, 64, 4096], P(('gx', 'gy', 'gz')), may hold values from -0.0546875 to 0.0546875
- counts: int32 [512], P(('gx', 'gy', 'gz')), may hold values from 16 to 64
- adjacency: int32 [512, 6], P(('gx', 'gy', 'gz')), may hold values from -1 to 511, as said below
- mat_id: int32 [512], replicated, may hold values from 0 to 15
- shear: float32 [16], replicated, may hold values from 0.25 to 4
- ratio: float32 [16], replicated, may hold values from 0.5 to 2
- owner_map: int32 [4, 128], P(('gx', 'gy')), may hold values from 0 to 127, each once within a row
Outputs:
- agglom: float32 [4, 128, 7, 4096], P(('gx', 'gy'), 'gz')
The draws below stay inside these ranges and needn't reach their ends.
Inputs may be any that keep to these rules, and one draw needn't show every extreme that they name: For each direction d, adjacency[i, 2 d + 1] = j names a subdomain of the next device along the d-th mesh axis (gx, gy, gz, device index (ix * 2 + iy) * 64 + iz holding subdomains index * 2 to index * 2 + 1) and then adjacency[j, 2 d] = i; -1 exactly where the device is the last (for 2 d + 1) or first (for 2 d) along that axis.
All inputs are finite; a program needn't handle non-finite values.
Results may differ from the reference program's by a relative error of at most 0.0003.
Values may be sent and summed in bfloat16 or wider, within the bound.
A program may use at most 192 MiB of HBM per device.

```python
import math
import jax
import jax.numpy as jnp
from jax import lax

NV = 64
SUB_DEV = 2
BX = 16
BY = 16
BZ = 16
NMAT = 16
CELLS = 4096
SUBS = 512
COL = 128
COLUMNS = 4
N_GX = 2
N_GY = 2
N_GZ = 64


def draw_adjacency(key, part):
    grid = (N_GX, N_GY, N_GZ, SUB_DEV)
    xpos = lax.broadcasted_iota(jnp.int32, grid, 0)
    ypos = lax.broadcasted_iota(jnp.int32, grid, 1)
    zpos = lax.broadcasted_iota(jnp.int32, grid, 2)
    local = lax.broadcasted_iota(jnp.int32, grid, 3)
    device = (xpos * N_GY + ypos) * N_GZ + zpos
    columns = []
    for axis, extent, stride, where_at in ((0, N_GX, N_GY * N_GZ, xpos), (1, N_GY, N_GZ, ypos), (2, N_GZ, 1, zpos)):
        scores = jax.random.randint(jax.random.fold_in(key, 17 + axis), grid, 0, 1 << 20)
        scores = scores * SUB_DEV + local
        forward = jnp.argsort(scores, axis=3, stable=True).astype(jnp.int32)
        backward = jnp.argsort(forward, axis=3, stable=True).astype(jnp.int32)
        before = jnp.roll(backward, 1, axis=axis)
        lower = jnp.where(where_at > 0, (device - stride) * SUB_DEV + before, -1)
        upper = jnp.where(where_at < extent - 1, (device + stride) * SUB_DEV + forward, -1)
        columns.append(lower)
        columns.append(upper)
    return jnp.stack(columns, -1).reshape(N_GX * N_GY * N_GZ * SUB_DEV, 6).astype(jnp.int32)


def place_ends(values, key, low, largest):
    spot = [jax.random.randint(jax.random.fold_in(key, axis), (), 0, length) for axis, length in enumerate(values.shape)]
    widest = values.shape.index(max(values.shape))
    next_to = spot[:widest] + [(spot[widest] + 1) % values.shape[widest]] + spot[widest + 1:]
    return values.at[tuple(spot)].set(low).at[tuple(next_to)].set(largest)


def shard_levels(key, shape, cuts, smallest, largest):
    def one(axis_at, parts):
        steps = jax.random.uniform(jax.random.fold_in(jax.random.fold_in(key, 6), axis_at), (parts,), jnp.float32, smallest / len(cuts), largest / len(cuts))
        return jnp.repeat(jnp.exp(steps), shape[axis_at] // parts).reshape((-1,) + (1,) * (len(shape) - axis_at - 1))

    level = one(*cuts[0])
    for cut in cuts[1:]:
        level = level * one(*cut)
    return level


def noise(own_key, shape, spread, bound, cuts=(), held_as=jnp.bfloat16):
    entries = jax.random.normal(own_key, shape, jnp.float32) * spread
    if len(cuts) > 0:
        entries = shard_levels(own_key, shape, cuts, -0.22, 0.18) * entries
    return jnp.clip(entries, min=-bound, max=bound).astype(held_as)


def setup_inputs(seed: int = 0) -> dict:
    seeds = jax.random.split(jax.random.key(seed), 8)
    return {
        "zvecs": noise(seeds[0], (SUBS, 3, NV, CELLS), (3 * CELLS) ** -0.5, 0.0546875, ((0, 256),)),
        "counts": place_ends(jax.random.randint(seeds[1], (SUBS,), NV // 4, NV + 1), jax.random.fold_in(seeds[1], 1), NV // 4, NV).astype(jnp.int32),
        "adjacency": draw_adjacency(jax.random.fold_in(seeds[7], 71), 0),
        "mat_id": place_ends(jax.random.randint(seeds[3], (SUBS,), 0, NMAT), jax.random.fold_in(seeds[3], 1), 0, NMAT - 1).astype(jnp.int32),
        "shear": jnp.clip(jnp.exp(jax.random.uniform(seeds[4], (NMAT,), jnp.float32, math.log(0.25), math.log(4.0))), 0.25, 4.0),
        "ratio": jnp.clip(jax.random.uniform(seeds[5], (NMAT,), jnp.float32, 0.5, 2.0), 0.5, 2.0),
        "owner_map": jax.vmap(lambda own: jax.random.permutation(own, COL))(jax.random.split(seeds[6], COLUMNS)).reshape((COLUMNS, COL)).astype(jnp.int32),
    }


def stencil(u, coef):
    cell = lax.iota(jnp.int32, BX * BY * BZ)
    zpos = cell % BZ
    ypos = cell // BZ % BY
    xpos = cell // (BY * BZ)
    plain = u.astype(jnp.float32)
    total = jnp.zeros(plain.shape, jnp.float32)
    lead = [(0, 0)] * (u.ndim - 1)
    for direction, stride, where_at, extent in ((0, BY * BZ, xpos, BX), (1, BZ, ypos, BY), (2, 1, zpos, BZ)):
        upper = jnp.pad(plain[..., stride:], lead + [(0, stride)])
        upper = jnp.where(where_at < extent - 1, upper, jnp.zeros((), jnp.float32))
        lower = jnp.pad(plain[..., :-stride], lead + [(stride, 0)])
        lower = jnp.where(where_at > 0, lower, jnp.zeros((), jnp.float32))
        total = total + coef[..., direction][..., None, None] * (2.0 * plain - upper - lower)
    return total

def face(u, direction, high):
    lead = u.shape[:-1]
    block = u.reshape(lead + (BX, BY, BZ))
    if direction == 0:
        return block[..., high * (BX - 1), :, :].reshape(lead + (BY * BZ,))
    if direction == 1:
        return block[..., :, high * (BY - 1), :].reshape(lead + (BX * BZ,))
    return block[..., :, :, high * (BZ - 1)].reshape(lead + (BX * BY,))

def coefficients(ids, shear, ratio):
    onehot = (ids[..., None] == lax.iota(jnp.int32, shear.shape[0])).astype(shear.dtype)
    modulus = lax.optimization_barrier(jnp.sum(onehot * shear, -1))
    excess = lax.optimization_barrier(jnp.sum(onehot * ratio, -1))
    unit = (lax.iota(jnp.int32, 3)[:, None] == lax.iota(jnp.int32, 3)[None, :]).astype(shear.dtype)
    return modulus[..., None, None] * (1.0 + excess[..., None, None] * unit)

def reference(zvecs, counts, adjacency, mat_id, shear, ratio, owner_map):
    vector_ids = lax.iota(jnp.int32, NV)

    def masked_of(index):
        keep = vector_ids < counts[index]
        return jnp.where(keep[None, :, None], zvecs[index], jnp.zeros((), zvecs.dtype))

    def one_row(index):
        own = masked_of(index)
        own_coef = coefficients(mat_id[index], shear, ratio)
        applied = stencil(own, own_coef).astype(jnp.bfloat16)
        blocks = [jnp.einsum('cvx,cwx->vw', own.astype(jnp.float32), applied.astype(jnp.float32))]
        for slot in range(6):
            direction = slot // 2
            high = slot % 2
            other = adjacency[index, slot]
            valid = (other >= 0).astype(jnp.float32)
            safe = jnp.maximum(other, 0)
            far = masked_of(safe)
            far_coef = coefficients(mat_id[safe], shear, ratio)
            weight = -jnp.sqrt(own_coef[:, direction] * far_coef[:, direction]) * valid
            near_face = face(own, direction, high).astype(jnp.float32)
            far_face = face(far, direction, 1 - high).astype(jnp.float32)
            blocks.append(jnp.einsum('c,cvx,cwx->vw', weight, near_face, far_face))
        return jnp.stack(blocks, 0).reshape(7, NV * NV)
    rows = lax.map(one_row, jnp.arange(SUBS, dtype=jnp.int32))
    rows = rows.reshape(COLUMNS, COL, 7, NV * NV)
    inverse = jnp.argsort(owner_map, axis=1).astype(jnp.int32)
    return jnp.take_along_axis(rows, inverse[:, :, None, None], axis=1)
```

```python
import jax
import jax.numpy as jnp
from jax import lax
from jax.sharding import PartitionSpec as P

BX = 16
BY = 16
BZ = 16


def extended(shard, sides, width):
    for axis, dim in sides:
        peers, length = (lax.axis_size(axis), shard.shape[dim])
        up = [(i, (i + 1) % peers) for i in range(peers - 1)]
        down = [(j, i) for i, j in up]
        last = lax.slice_in_dim(shard, length - width, length, axis=dim)
        initial = lax.slice_in_dim(shard, 0, width, axis=dim)
        before = lax.ppermute(last, axis, up)
        after = lax.ppermute(initial, axis, down)
        shard = jnp.concatenate([before, shard, after], axis=dim)
    return shard


def stencil(u, coef):
    cell = lax.iota(jnp.int32, BX * BY * BZ)
    zpos = cell % BZ
    ypos = cell // BZ % BY
    xpos = cell // (BY * BZ)
    plain = u.astype(jnp.float32)
    total = jnp.zeros(plain.shape, jnp.float32)
    lead = [(0, 0)] * (u.ndim - 1)
    for direction, stride, where_at, extent in (
        (0, BY * BZ, xpos, BX),
        (1, BZ, ypos, BY),
        (2, 1, zpos, BZ),
    ):
        upper = jnp.pad(plain[..., stride:], lead + [(0, stride)])
        upper = jnp.where(where_at < extent - 1, upper, jnp.zeros((), jnp.float32))
        lower = jnp.pad(plain[..., :-stride], lead + [(stride, 0)])
        lower = jnp.where(where_at > 0, lower, jnp.zeros((), jnp.float32))
        total = total + coef[..., direction][..., None, None] * (2.0 * plain - upper - lower)
    return total


def face(u, direction, high):
    lead = u.shape[:-1]
    block = u.reshape(lead + (BX, BY, BZ))
    if direction == 0:
        return block[..., high * (BX - 1), :, :].reshape(lead + (BY * BZ,))
    if direction == 1:
        return block[..., :, high * (BY - 1), :].reshape(lead + (BX * BZ,))
    return block[..., :, :, high * (BZ - 1)].reshape(lead + (BX * BY,))


def coefficients(ids, shear, ratio):
    onehot = (ids[..., None] == lax.iota(jnp.int32, shear.shape[0])).astype(jnp.float32)
    modulus = jnp.sum(onehot * shear, -1)
    excess = jnp.sum(onehot * ratio, -1)
    unit = (lax.iota(jnp.int32, 3)[:, None] == lax.iota(jnp.int32, 3)[None, :]).astype(jnp.float32)
    return modulus[..., None, None] * (1.0 + excess[..., None, None] * unit)


def neighbour_layers(both, direction):
    if direction == 0:
        return extended(both, (("gx", 0),), 1)
    if direction == 1:
        return extended(both, (("gy", 0),), 1)
    return extended(both, (("gz", 0),), 1)


def per_device(zvecs, counts, adjacency, mat_id, shear, ratio, owner_map):
    subs = zvecs.shape[0]
    nvec = zvecs.shape[2]
    keep = lax.iota(jnp.int32, nvec)[None, :] < counts[:, None]
    masked = jnp.where(keep[:, None, :, None], zvecs, jnp.zeros((), zvecs.dtype))
    device = lax.axis_index(("gx", "gy", "gz"))
    own_ids = lax.dynamic_slice_in_dim(mat_id, device * subs, subs)
    coef = coefficients(own_ids, shear, ratio)
    applied = stencil(masked, coef).astype(jnp.bfloat16)
    blocks = [jnp.einsum("scvx,scwx->svw", masked, applied, preferred_element_type=jnp.float32)]
    valid = (adjacency >= 0).astype(jnp.float32)
    local = jnp.where(adjacency >= 0, adjacency % subs, 0)
    far_coef = coefficients(jnp.take(mat_id, jnp.maximum(adjacency, 0)), shear, ratio)

    def couple(near_face, far_face, slot):
        direction = slot // 2
        weight = (
            -jnp.sqrt(coef[:, :, direction] * far_coef[:, slot, :, direction])
            * valid[:, slot : slot + 1]
        )
        inner = jnp.einsum(
            "scvx,scwx->scvw", near_face, far_face, preferred_element_type=jnp.float32
        )
        return jnp.sum(weight[:, :, None, None] * inner, 1)

    for direction in range(3):
        both = jnp.stack([face(masked, direction, 0), face(masked, direction, 1)], 0)
        padded = neighbour_layers(both, direction)
        below = jnp.take(padded[0], local[:, 2 * direction], axis=0)
        above = jnp.take(padded[3], local[:, 2 * direction + 1], axis=0)
        blocks.append(couple(both[0], below, 2 * direction))
        blocks.append(couple(both[1], above, 2 * direction + 1))
    rows = jnp.stack(blocks, 1)
    peers = lax.axis_size("gz")
    lines = nvec // peers
    cut = rows.reshape(subs, 7, peers, lines * nvec).transpose(2, 1, 0, 3).reshape(peers, 7, subs * lines * nvec)
    spread = lax.all_to_all(cut, "gz", split_axis=0, concat_axis=0, tiled=True)
    spread = spread.reshape(peers, 7, subs, lines * nvec).transpose(0, 2, 1, 3).reshape(peers * subs, 7, lines * nvec)
    column = owner_map[0]
    places = lax.iota(jnp.int32, column.shape[0])
    inverse = jnp.sum(jnp.where(column[None, :] == places[:, None], places[None, :], 0), 1)
    owned = jnp.take(spread, inverse, axis=0, mode="clip")
    owned = owned.reshape(peers, subs, 7, lines * nvec).transpose(0, 2, 1, 3).reshape(peers, 7, subs * lines * nvec)
    arrived = lax.all_to_all(owned, "gz", split_axis=0, concat_axis=0, tiled=True)
    agglom = arrived.reshape(peers, 7, subs, lines * nvec).transpose(2, 1, 0, 3).reshape(1, subs, 7, nvec * nvec)
    return agglom


def solution(mesh):
    placed = (
        P(("gx", "gy", "gz"), None, None, None),
        P(("gx", "gy", "gz")),
        P(("gx", "gy", "gz"), None),
        P(),
        P(),
        P(),
        P(("gx", "gy"), None),
    )
    return jax.shard_map(
        per_device,
        mesh=mesh,
        in_specs=placed,
        out_specs=P(("gx", "gy"), "gz", None, None),
        check_vma=False,
    )
```

```python
import functools

import jax
import jax.numpy as jnp
from jax import lax
from jax.experimental import pallas as pl
from jax.experimental.pallas import tpu as pltpu
from jax.sharding import PartitionSpec as P

BX = 16
SLAB = 256
CELLS = 4096
NV = 64
ROWS = 128
PEERS = 64
LANES = 128
GROUP = 4
MESH = pl.DeviceIdType.MESH
F32 = jnp.float32
BF16 = jnp.bfloat16
TRANS = (((1,), (1,)), ((), ()))


def iota(shape, dim):
    return lax.broadcasted_iota(jnp.int32, shape, dim)


def picked(flag):
    return jnp.where(flag, 1.0, 0.0).astype(BF16)


def by_sub(first, second, shape):
    return jnp.where(iota(shape, len(shape) - 1) < NV, first, second)


def kernel(
    zvecs, counts, adjacency, mat_id, shear, ratio, owner,
    out,
    u, weave, select, faces, far, send1, recv1, send2, recv2,
    load_sem, face_send, face_recv, a2a_send, a2a_recv,
):
    gx, gy, gz = lax.axis_index("gx"), lax.axis_index("gy"), lax.axis_index("gz")
    device = (gx * 2 + gy) * PEERS + gz

    loads = []
    for c in range(3):
        for s in range(2):
            loads.append(
                pltpu.make_async_copy(
                    zvecs.at[s, c],
                    u.at[c, pl.ds(s * NV, NV), pl.ds(SLAB, CELLS)],
                    load_sem.at[c, s],
                )
            )
            loads[-1].start()

    barrier = pltpu.get_barrier_semaphore()
    pl.semaphore_signal(barrier, inc=1, device_id={"gx": 1 - gx}, device_id_type=MESH)
    pl.semaphore_signal(barrier, inc=1, device_id={"gy": 1 - gy}, device_id_type=MESH)

    def greet(k, carry):
        pl.semaphore_signal(
            barrier, inc=1, device_id={"gz": lax.rem(gz + k, PEERS)}, device_id_type=MESH
        )
        return carry

    lax.fori_loop(1, PEERS, greet, 0)

    col = iota((1, LANES), 1)
    base = (col // BX) * SLAB
    inner = col % BX
    targets = (base + (1 - gy) * 15 * BX + inner, base + inner * BX, base + inner * BX + 15)

    def fill(k, carry):
        row = iota((SLAB, LANES), 0) + k * SLAB
        for f in range(3):
            select[pl.ds(pl.multiple_of(k * SLAB, SLAB), SLAB), f * LANES : (f + 1) * LANES] = picked(
                row == targets[f]
            )
        return carry

    lax.fori_loop(0, 8, fill, 0)

    row = iota((SLAB, SLAB), 0)
    cell = iota((SLAB, SLAB), 1)
    zpos = cell % BX
    diag = jnp.where(row == cell, 2.0, 0.0)
    along_y = diag - jnp.where((row == cell + BX) | (row == cell - BX), 1.0, 0.0)
    along_z = diag - jnp.where(
        ((row == cell + 1) & (zpos < BX - 1)) | ((row == cell - 1) & (zpos > 0)), 1.0, 0.0
    )
    weave[:, 0:SLAB] = (along_y + along_z).astype(BF16)
    weave[:, SLAB : 2 * SLAB] = along_y.astype(BF16)
    weave[:, 2 * SLAB : 3 * SLAB] = along_z.astype(BF16)

    rows_of = iota((ROWS, 1), 0)
    used = jnp.where(rows_of < NV, counts[0], counts[1] + NV)
    keep = jnp.where(rows_of < used, 1.0, 0.0)

    zero_slab = jnp.zeros((ROWS, SLAB), BF16)
    near_x = (1 - gx) * 15 + 1
    for c in range(3):
        u[c, :, 0:SLAB] = zero_slab
        u[c, :, SLAB + CELLS : 2 * SLAB + CELLS] = zero_slab
        loads[2 * c].wait()
        loads[2 * c + 1].wait()
        for h in range(2):
            got = jnp.dot(
                u[c, :, SLAB + h * 2048 : SLAB + (h + 1) * 2048],
                select[...],
                preferred_element_type=F32,
            )
            got = (got * keep).astype(BF16)
            for f in range(3):
                faces[f + 1, c, :, h * LANES : (h + 1) * LANES] = got[:, f * LANES : (f + 1) * LANES]
        edge = u[c, :, pl.ds(pl.multiple_of(near_x * SLAB, SLAB), SLAB)].astype(F32)
        faces[0, c] = (edge * keep).astype(BF16)

    pl.semaphore_wait(barrier, PEERS + 1)
    moves = []
    for slot, source, target in (
        (1, 1, {"gy": 1 - gy}),
        (2, 3, {"gz": lax.rem(gz + 1, PEERS)}),
        (0, 0, {"gx": 1 - gx}),
    ):
        moves.append(
            pltpu.make_async_remote_copy(
                src_ref=faces.at[source],
                dst_ref=far.at[slot],
                send_sem=face_send.at[slot],
                recv_sem=face_recv.at[slot],
                device_id=target,
                device_id_type=MESH,
            )
        )
        moves[-1].start()

    own = [mat_id[device * 2 + s] for s in range(2)]
    own_shear = [shear[m] for m in own]
    own_ratio = [ratio[m] for m in own]
    by_row = rows_of < NV
    scale = jnp.where(by_row, own_shear[0], own_shear[1])
    extra = jnp.where(by_row, own_shear[0] * own_ratio[0], own_shear[1] * own_ratio[1])

    total = jnp.zeros((ROWS, ROWS), F32)
    for c in range(3):

        def group(g, total, c=c):
            start = pl.multiple_of(g * (GROUP * SLAB), GROUP * SLAB)
            slabs = [u[c, :, pl.ds(start + i * SLAB, SLAB)] for i in range(GROUP + 2)]
            stacked = jnp.concatenate(slabs[1:-1], axis=0)
            flat = jnp.dot(stacked, weave[:, 0:SLAB], preferred_element_type=F32)
            if c > 0:
                lone = jnp.dot(
                    stacked, weave[:, c * SLAB : (c + 1) * SLAB], preferred_element_type=F32
                )
            for i in range(GROUP):
                lower, here, upper = [slabs[i + k].astype(F32) for k in range(3)]
                along_x = 2.0 * here - upper - lower
                rest = flat[i * ROWS : (i + 1) * ROWS]
                special = along_x if c == 0 else lone[i * ROWS : (i + 1) * ROWS]
                applied = (scale * (along_x + rest) + extra * special).astype(BF16)
                total = total + lax.dot_general(
                    slabs[i + 1], applied, TRANS, preferred_element_type=F32
                )
            return total

        total = lax.fori_loop(0, BX // GROUP, group, total)

    shape = (NV, LANES)
    v_of = iota(shape, 0)
    w_of = iota(shape, 1)
    limit = by_sub(counts[0], counts[1], shape)
    inside = (v_of < limit) & (lax.rem(w_of, NV) < limit)
    block = by_sub(total[0:NV], total[NV:ROWS], shape)
    send1[pl.ds(0, NV, stride=8), :] = jnp.where(inside, block, 0.0)

    def couple(left, right, weights):
        result = None
        for c in range(3):
            full = lax.dot_general(left(c), right(c), TRANS, preferred_element_type=F32)
            result = weights[c] * full if result is None else result + weights[c] * full
        return result

    def matched(full, swap):
        turned = pltpu.roll(full, NV, 1)
        return by_sub(
            jnp.where(swap[0], turned[0:NV], full[0:NV]),
            jnp.where(swap[1], turned[NV:ROWS], full[NV:ROWS]),
            shape,
        )

    def pairing(slot, direction):
        swap, values = [], []
        for s in range(2):
            other = adjacency[s, slot]
            there = mat_id[jnp.maximum(other, 0)]
            there_shear, there_ratio = shear[there], ratio[there]
            other = jnp.full((1, LANES), other, jnp.int32)
            swap.append((other >= 0) & ((other & 1) != s))
            valid = jnp.where(other >= 0, -1.0, 0.0)
            line = []
            for c in range(3):
                unit = 1.0 if c == direction else 0.0
                product = (own_shear[s] * (1.0 + own_ratio[s] * unit)) * (
                    there_shear * (1.0 + there_ratio * unit)
                )
                line.append(valid * jnp.sqrt(jnp.full((1, LANES), product, F32)))
            values.append(line)
        return swap, values

    for order, (direction, slot, near, line) in enumerate(
        ((0, 1 - gx, 0, 1), (1, 3 - gy, 1, 2), (2, 4, 2, 3))
    ):
        swap, values = pairing(slot, direction)
        moves[(2, 0, 1)[order]].wait_recv()
        weights = [jnp.where(by_row, values[0][c], values[1][c]) for c in range(3)]
        full = couple(lambda c: faces[near, c], lambda c: far[direction, c], weights)
        send1[pl.ds(line, NV, stride=8), :] = matched(full, swap)
        if direction == 2:
            weights = [by_sub(values[0][c], values[1][c], (1, LANES)) for c in range(3)]
            full = couple(lambda c: far[2, c], lambda c: faces[2, c], weights)
            send1[pl.ds(4, NV, stride=8), :] = matched(full, swap)
    for move in moves:
        move.wait_send()

    def exchange(phase, source, target):
        def post(k, carry):
            peer = lax.rem(gz + k, PEERS)
            pltpu.make_async_remote_copy(
                src_ref=source.at[pl.ds(pl.multiple_of(peer * 8, 8), TILE)],
                dst_ref=target.at[pl.ds(pl.multiple_of(gz * 8, 8), TILE)],
                send_sem=a2a_send.at[phase],
                recv_sem=a2a_recv.at[phase],
                device_id={"gz": peer},
                device_id_type=MESH,
            ).start()
            return carry

        lax.fori_loop(1, PEERS, post, 0)
        mine = pl.ds(pl.multiple_of(gz * 8, 8), 8)
        target[mine, :] = source[mine, :]

    def arrive(phase, source, target):
        size = (PEERS - 1) * TILE
        whole = pltpu.make_async_remote_copy(
            src_ref=source.at[pl.ds(0, size)],
            dst_ref=target.at[pl.ds(0, size)],
            send_sem=a2a_send.at[phase],
            recv_sem=a2a_recv.at[phase],
            device_id={"gz": lax.rem(gz + 1, PEERS)},
            device_id_type=MESH,
        )
        whole.wait_recv()
        whole.wait_send()

    exchange(0, send1, recv1)

    line = iota((ROWS, ROWS), 0)
    spot = iota((ROWS, ROWS), 1)
    half = spot // NV
    holder = lax.rem(spot, NV)
    places = owner[...].astype(F32).astype(BF16)
    places = jnp.broadcast_to(places, (8, ROWS))
    want = (2 * lax.rem(line, NV) + line // NV).astype(F32)

    def moved(shift):
        sub = 2 * lax.rem(holder + (PEERS - shift), PEERS) + half
        place = jnp.dot(places, picked(line == sub), preferred_element_type=F32)
        hit = picked(place[0:1, :] == want)
        return jnp.concatenate([hit, hit, hit], axis=1)

    straight, shifted = moved(0), moved(1)
    arrive(0, send1, recv1)
    for b in range(5):
        chunk = recv1[pl.ds(b, PEERS, stride=8), :]
        turned = pltpu.roll(chunk, NV, 1)
        chunk = jnp.concatenate(
            [by_sub(chunk, turned, shape), by_sub(turned, chunk, shape)], axis=0
        )
        high = chunk.astype(BF16)
        left = chunk - high.astype(F32)
        middle = left.astype(BF16)
        low = (left - middle.astype(F32)).astype(BF16)
        full = jnp.dot(
            shifted if b == 4 else straight,
            jnp.concatenate([high, middle, low], axis=0),
            preferred_element_type=F32,
        )
        send2[pl.ds(b, PEERS, stride=8), :] = by_sub(full[0:NV], full[NV:ROWS], shape)

    exchange(1, send2, recv2)
    tile = (8, LANES)
    b_of = iota(tile, 0)
    x_at, y_at = 2 - gx, 4 - gy
    plain = (b_of == 0) | ((b_of == x_at) & (gx == 1))
    once = ((b_of == x_at) & (gx == 0)) | ((b_of == y_at) & (gy == 1))
    twice = ((b_of == y_at) & (gy == 0)) | (b_of > 4)
    arrive(1, send2, recv2)

    def place(m, carry):
        pair = [recv2[pl.ds(pl.multiple_of((2 * m + i) * 8, 8), 8), :] for i in range(2)]
        turned = [pltpu.roll(t, NV, 1) for t in pair]
        for p, value in enumerate(
            (by_sub(pair[0], turned[1], tile), by_sub(turned[0], pair[1], tile))
        ):
            value = jnp.where(
                plain,
                value,
                jnp.where(
                    once,
                    pltpu.roll(value, 1, 0),
                    jnp.where(twice, pltpu.roll(value, 2, 0), 0.0),
                ),
            )
            out[p, :, pl.ds(pl.multiple_of(m * LANES, LANES), LANES)] = value[0:7]
        return carry

    lax.fori_loop(0, CELLS // LANES, place, 0, unroll=4)


TILE = 5


def per_device(zvecs, counts, adjacency, mat_id, shear, ratio, owner_map):
    smem = pl.BlockSpec(memory_space=pltpu.SMEM)
    vmem = pl.BlockSpec(memory_space=pltpu.VMEM)
    rows = pl.pallas_call(
        kernel,
        out_shape=jax.ShapeDtypeStruct((2, 7, CELLS), F32),
        in_specs=[pl.BlockSpec(memory_space=pl.ANY), smem, smem, smem, smem, smem, vmem],
        out_specs=vmem,
        scratch_shapes=[
            pltpu.VMEM((3, ROWS, CELLS + 2 * SLAB), BF16),
            pltpu.VMEM((SLAB, 3 * SLAB), BF16),
            pltpu.VMEM((8 * SLAB, 3 * LANES), BF16),
            pltpu.VMEM((4, 3, ROWS, SLAB), BF16),
            pltpu.VMEM((3, 3, ROWS, SLAB), BF16),
            pltpu.VMEM((PEERS * 8, LANES), F32),
            pltpu.VMEM((PEERS * 8, LANES), F32),
            pltpu.VMEM((PEERS * 8, LANES), F32),
            pltpu.VMEM((PEERS * 8, LANES), F32),
            pltpu.SemaphoreType.DMA((3, 2)),
            pltpu.SemaphoreType.DMA((3,)),
            pltpu.SemaphoreType.DMA((3,)),
            pltpu.SemaphoreType.DMA((2,)),
            pltpu.SemaphoreType.DMA((2,)),
        ],
        compiler_params=pltpu.CompilerParams(collective_id=0, has_side_effects=True),
        name="assemble",
    )(zvecs, counts, adjacency, mat_id, shear, ratio, owner_map)
    return rows[None]


def solution(mesh):
    placed = (
        P(("gx", "gy", "gz"), None, None, None),
        P(("gx", "gy", "gz")),
        P(("gx", "gy", "gz"), None),
        P(),
        P(),
        P(),
        P(("gx", "gy"), None),
    )
    return jax.shard_map(
        per_device,
        mesh=mesh,
        in_specs=placed,
        out_specs=P(("gx", "gy"), "gz", None, None),
        check_vma=False,
    )
```

```python
import functools

import jax
import jax.numpy as jnp
from jax import lax
from jax.experimental import pallas as pl
from jax.experimental.pallas import tpu as pltpu
from jax.sharding import PartitionSpec as P

BX = 16
SLAB = 256
CELLS = 4096
NV = 64
ROWS = 128
PEERS = 64
LANES = 128
GROUP = 4
MESH = pl.DeviceIdType.MESH
F32 = jnp.float32
BF16 = jnp.bfloat16
TRANS = (((1,), (1,)), ((), ()))


def iota(shape, dim):
    return lax.broadcasted_iota(jnp.int32, shape, dim)


def picked(flag):
    return jnp.where(flag, 1.0, 0.0).astype(BF16)


def by_sub(first, second, shape):
    return jnp.where(iota(shape, len(shape) - 1) < NV, first, second)


def kernel(
    zvecs, counts, adjacency, mat_id, shear, ratio, owner,
    out,
    u, weave, select, near, far, near_y, far_y, back_out, back_in, send1, recv1, send2, recv2,
    load_sem, face_send, face_recv, back_sem, a2a_send, a2a_recv, ring_sem,
):
    gx, gy, gz = lax.axis_index("gx"), lax.axis_index("gy"), lax.axis_index("gz")
    device = (gx * 2 + gy) * PEERS + gz

    loads = []
    for c in range(3):
        for s in range(2):
            loads.append(
                pltpu.make_async_copy(
                    zvecs.at[s, c],
                    u.at[c, pl.ds(s * NV, NV), pl.ds(SLAB, CELLS)],
                    load_sem.at[c, s],
                )
            )
            loads[-1].start()

    barrier = pltpu.get_barrier_semaphore()
    pl.semaphore_signal(barrier, inc=1, device_id={"gx": 1 - gx}, device_id_type=MESH)
    pl.semaphore_signal(barrier, inc=1, device_id={"gy": 1 - gy}, device_id_type=MESH)

    plane, spot = gz // 8, lax.rem(gz, 8)
    above = lax.rem(plane + 1, 8) * 8 + spot
    below = lax.rem(plane + 7, 8) * 8 + spot
    for peer in [lax.rem(gz + 1, PEERS), lax.rem(gz + PEERS - 1, PEERS), above, below] + [
        plane * 8 + lax.rem(spot + k, 8) for k in range(1, 8)
    ]:
        pl.semaphore_signal(barrier, inc=1, device_id={"gz": peer}, device_id_type=MESH)

    def pass_on(step):
        if step > 0:
            pl.semaphore_wait(ring_sem.at[0], 1)
        if step < 4:
            pl.semaphore_signal(
                ring_sem.at[0], inc=1, device_id={"gz": above}, device_id_type=MESH
            )
        if 0 < step < 4:
            pl.semaphore_wait(ring_sem.at[1], 1)
        if step < 3:
            pl.semaphore_signal(
                ring_sem.at[1], inc=1, device_id={"gz": below}, device_id_type=MESH
            )

    col = iota((1, LANES), 1)
    base = (col // BX) * SLAB
    inner = col % BX
    targets = (base + (1 - gy) * 15 * BX + inner, base + inner * BX, base + inner * BX + 15)

    def fill(k, carry):
        row = iota((SLAB, LANES), 0) + k * SLAB
        for f in range(3):
            select[pl.ds(pl.multiple_of(k * SLAB, SLAB), SLAB), f * LANES : (f + 1) * LANES] = picked(
                row == targets[f]
            )
        return carry

    lax.fori_loop(0, 8, fill, 0)

    row = iota((SLAB, SLAB), 0)
    cell = iota((SLAB, SLAB), 1)
    zpos = cell % BX
    diag = jnp.where(row == cell, 2.0, 0.0)
    along_y = diag - jnp.where((row == cell + BX) | (row == cell - BX), 1.0, 0.0)
    along_z = diag - jnp.where(
        ((row == cell + 1) & (zpos < BX - 1)) | ((row == cell - 1) & (zpos > 0)), 1.0, 0.0
    )
    weave[:, 0:SLAB] = (along_y + along_z).astype(BF16)
    weave[:, SLAB : 2 * SLAB] = along_y.astype(BF16)
    weave[:, 2 * SLAB : 3 * SLAB] = along_z.astype(BF16)

    rows_of = iota((ROWS, 1), 0)
    used = jnp.where(rows_of < NV, counts[0], counts[1] + NV)
    keep = jnp.where(rows_of < used, 1.0, 0.0)

    swapped = jnp.full((1, SLAB), adjacency[0, 3 - gy] & 1, jnp.int32)
    keep_last = (swapped + (1 - gy)) > 0

    zero_slab = jnp.zeros((ROWS, SLAB), BF16)
    near_x = (1 - gx) * 15 + 1
    moves = [[], [], []]
    for c in range(3):
        u[c, :, 0:SLAB] = zero_slab
        u[c, :, SLAB + CELLS : 2 * SLAB + CELLS] = zero_slab
        loads[2 * c].wait()
        loads[2 * c + 1].wait()
        parts = []
        for h in range(2):
            got = jnp.dot(
                u[c, :, SLAB + h * 2048 : SLAB + (h + 1) * 2048],
                select[...],
                preferred_element_type=F32,
            )
            parts.append(got * keep)
        layers = [
            jnp.concatenate([p[:, f * LANES : (f + 1) * LANES] for p in parts], axis=1)
            for f in range(3)
        ]
        near_y[0, c] = jnp.where(keep_last, layers[0][NV:ROWS], layers[0][0:NV]).astype(BF16)
        near_y[1, c] = jnp.where(keep_last, layers[0][0:NV], layers[0][NV:ROWS]).astype(BF16)
        near[1, c] = layers[1].astype(BF16)
        near[2, c] = layers[2].astype(BF16)
        edge = u[c, :, pl.ds(pl.multiple_of(near_x * SLAB, SLAB), SLAB)].astype(F32)
        near[0, c] = (edge * keep).astype(BF16)
        if c == 0:
            pl.semaphore_wait(barrier, 13)
            pass_on(0)
        for slot, source, landing, target in (
            (1, near_y.at[1, c], far_y.at[c], {"gy": 1 - gy}),
            (2, near.at[2, c], far.at[1, c], {"gz": lax.rem(gz + 1, PEERS)}),
            (0, near.at[0, c], far.at[0, c], {"gx": 1 - gx}),
        ):
            move = pltpu.make_async_remote_copy(
                src_ref=source,
                dst_ref=landing,
                send_sem=face_send.at[slot, c],
                recv_sem=face_recv.at[slot, c],
                device_id=target,
                device_id_type=MESH,
            )
            move.start()
            moves[slot].append(move)

    own = [mat_id[device * 2 + s] for s in range(2)]
    own_shear = [shear[m] for m in own]
    own_ratio = [ratio[m] for m in own]
    by_row = rows_of < NV
    scale = jnp.where(by_row, own_shear[0], own_shear[1])
    extra = jnp.where(by_row, own_shear[0] * own_ratio[0], own_shear[1] * own_ratio[1])

    def stencil(c, total):
        def group(g, total):
            start = pl.multiple_of(g * (GROUP * SLAB), GROUP * SLAB)
            slabs = [u[c, :, pl.ds(start + i * SLAB, SLAB)] for i in range(GROUP + 2)]
            stacked = jnp.concatenate(slabs[1:-1], axis=0)
            flat = jnp.dot(stacked, weave[:, 0:SLAB], preferred_element_type=F32)
            if c > 0:
                lone = jnp.dot(
                    stacked, weave[:, c * SLAB : (c + 1) * SLAB], preferred_element_type=F32
                )
            for i in range(GROUP):
                lower, here, upper = [slabs[i + k].astype(F32) for k in range(3)]
                along_x = 2.0 * here - upper - lower
                rest = flat[i * ROWS : (i + 1) * ROWS]
                special = along_x if c == 0 else lone[i * ROWS : (i + 1) * ROWS]
                applied = (scale * (along_x + rest) + extra * special).astype(BF16)
                total = total + lax.dot_general(
                    slabs[i + 1], applied, TRANS, preferred_element_type=F32
                )
            return total

        return lax.fori_loop(0, BX // GROUP, group, total)

    shape = (NV, LANES)

    def couple(left, right, weights):
        result = None
        for c in range(3):
            full = lax.dot_general(left(c), right(c), TRANS, preferred_element_type=F32)
            result = weights[c] * full if result is None else result + weights[c] * full
        return result

    def matched(full, swap):
        turned = pltpu.roll(full, NV, 1)
        return by_sub(
            jnp.where(swap[0], turned[0:NV], full[0:NV]),
            jnp.where(swap[1], turned[NV:ROWS], full[NV:ROWS]),
            shape,
        )

    def pairing(slot, direction):
        swap, values = [], []
        for s in range(2):
            other = adjacency[s, slot]
            there = mat_id[jnp.maximum(other, 0)]
            there_shear, there_ratio = shear[there], ratio[there]
            other = jnp.full((1, LANES), other, jnp.int32)
            swap.append((other >= 0) & ((other & 1) != s))
            valid = jnp.where(other >= 0, -1.0, 0.0)
            line = []
            for c in range(3):
                unit = 1.0 if c == direction else 0.0
                product = (own_shear[s] * (1.0 + own_ratio[s] * unit)) * (
                    there_shear * (1.0 + there_ratio * unit)
                )
                line.append(valid * jnp.sqrt(jnp.full((1, LANES), product, F32)))
            values.append(line)
        return swap, values

    pass_on(1)
    total = stencil(0, jnp.zeros((ROWS, ROWS), F32))
    pass_on(2)
    total = stencil(1, total)
    pass_on(3)

    _, values = pairing(3 - gy, 1)
    keep_here = keep_last[:, 0:LANES]
    weights = [jnp.where(keep_here, values[1][c], values[0][c]) for c in range(3)]
    for move in moves[1]:
        move.wait_recv()
    twice = lambda ref, c: jnp.concatenate([ref[c], ref[c]], axis=0)
    kept = couple(lambda c: near_y[0, c], lambda c: twice(far_y, c), weights)
    other = couple(lambda c: far_y[c], lambda c: twice(near_y.at[0], c), weights)
    back_out[...] = by_sub(other[0 : NV // 2], other[NV // 2 : NV], (NV // 2, LANES))
    back = pltpu.make_async_remote_copy(
        src_ref=back_out,
        dst_ref=back_in,
        send_sem=back_sem.at[0],
        recv_sem=back_sem.at[1],
        device_id={"gy": 1 - gy},
        device_id_type=MESH,
    )
    back.start()

    total = stencil(2, total)
    v_of = iota(shape, 0)
    w_of = iota(shape, 1)
    limit = by_sub(counts[0], counts[1], shape)
    inside = (v_of < limit) & (lax.rem(w_of, NV) < limit)
    block = by_sub(total[0:NV], total[NV:ROWS], shape)
    send1[pl.ds(0, NV, stride=8), :] = jnp.where(inside, block, 0.0)

    swap, values = pairing(1 - gx, 0)
    for move in moves[0]:
        move.wait_recv()
    weights = [jnp.where(by_row, values[0][c], values[1][c]) for c in range(3)]
    full = couple(lambda c: near[0, c], lambda c: far[0, c], weights)
    send1[pl.ds(1, NV, stride=8), :] = matched(full, swap)

    back.wait_recv()
    packed = back_in[...]
    turned = pltpu.roll(packed, NV, 1)
    given = jnp.concatenate(
        [by_sub(packed, turned, packed.shape), by_sub(turned, packed, packed.shape)], axis=0
    )
    send1[pl.ds(2, NV, stride=8), :] = by_sub(
        jnp.where(keep_here, given, kept), jnp.where(keep_here, kept, given), shape
    )

    swap, values = pairing(4, 2)
    for move in moves[2]:
        move.wait_recv()
    weights = [jnp.where(by_row, values[0][c], values[1][c]) for c in range(3)]
    full = couple(lambda c: near[1, c], lambda c: far[1, c], weights)
    send1[pl.ds(3, NV, stride=8), :] = matched(full, swap)
    weights = [by_sub(values[0][c], values[1][c], (1, LANES)) for c in range(3)]
    full = couple(lambda c: far[1, c], lambda c: near[1, c], weights)
    send1[pl.ds(4, NV, stride=8), :] = matched(full, swap)

    def exchange(phase, source, target):
        def post(k, carry):
            ring = k // 8
            step = (ring + 1) // 2
            ring = PEERS // 16 + step * (2 * lax.rem(ring, 2) - 1)
            peer = lax.rem(gz // 8 + ring, 8) * 8 + lax.rem(gz + k + 1, 8)
            pltpu.make_async_remote_copy(
                src_ref=source.at[pl.ds(pl.multiple_of(peer * 8, 8), TILE)],
                dst_ref=target.at[pl.ds(pl.multiple_of(gz * 8, 8), TILE)],
                send_sem=a2a_send.at[phase],
                recv_sem=a2a_recv.at[phase],
                device_id={"gz": peer},
                device_id_type=MESH,
            ).start()
            return carry

        lax.fori_loop(0, PEERS - 1, post, 0)
        mine = pl.ds(pl.multiple_of(gz * 8, 8), 8)
        target[mine, :] = source[mine, :]

    def whole(phase, source, target):
        size = (PEERS - 1) * TILE
        return pltpu.make_async_remote_copy(
            src_ref=source.at[pl.ds(0, size)],
            dst_ref=target.at[pl.ds(0, size)],
            send_sem=a2a_send.at[phase],
            recv_sem=a2a_recv.at[phase],
            device_id={"gz": lax.rem(gz + 1, PEERS)},
            device_id_type=MESH,
        )

    pass_on(4)
    exchange(0, send1, recv1)

    line = iota((ROWS, ROWS), 0)
    spot = iota((ROWS, ROWS), 1)
    half = spot // NV
    holder = lax.rem(spot, NV)
    places = owner[...].astype(F32).astype(BF16)
    places = jnp.broadcast_to(places, (8, ROWS))
    want = (2 * lax.rem(line, NV) + line // NV).astype(F32)

    def moved(shift):
        sub = 2 * lax.rem(holder + (PEERS - shift), PEERS) + half
        place = jnp.dot(places, picked(line == sub), preferred_element_type=F32)
        hit = picked(place[0:1, :] == want)
        return jnp.concatenate([hit, hit, hit], axis=1)

    straight, shifted = moved(0), moved(1)
    whole(0, send1, recv1).wait_recv()
    for b in range(5):
        chunk = recv1[pl.ds(b, PEERS, stride=8), :]
        turned = pltpu.roll(chunk, NV, 1)
        chunk = jnp.concatenate(
            [by_sub(chunk, turned, shape), by_sub(turned, chunk, shape)], axis=0
        )
        high = chunk.astype(BF16)
        left = chunk - high.astype(F32)
        middle = left.astype(BF16)
        low = (left - middle.astype(F32)).astype(BF16)
        full = jnp.dot(
            shifted if b == 4 else straight,
            jnp.concatenate([high, middle, low], axis=0),
            preferred_element_type=F32,
        )
        send2[pl.ds(b, PEERS, stride=8), :] = by_sub(full[0:NV], full[NV:ROWS], shape)

    exchange(1, send2, recv2)
    tile = (8, LANES)
    b_of = iota(tile, 0)
    x_at, y_at = 2 - gx, 4 - gy
    plain = (b_of == 0) | ((b_of == x_at) & (gx == 1))
    once = ((b_of == x_at) & (gx == 0)) | ((b_of == y_at) & (gy == 1))
    twice = ((b_of == y_at) & (gy == 0)) | (b_of > 4)
    whole(1, send2, recv2).wait_recv()

    def place(m, carry):
        pair = [recv2[pl.ds(pl.multiple_of((2 * m + i) * 8, 8), 8), :] for i in range(2)]
        turned = [pltpu.roll(t, NV, 1) for t in pair]
        for p, value in enumerate(
            (by_sub(pair[0], turned[1], tile), by_sub(turned[0], pair[1], tile))
        ):
            value = jnp.where(
                plain,
                value,
                jnp.where(
                    once,
                    pltpu.roll(value, 1, 0),
                    jnp.where(twice, pltpu.roll(value, 2, 0), 0.0),
                ),
            )
            out[:, p, pl.ds(pl.multiple_of(m * LANES, LANES), LANES)] = value[0:7]
        return carry

    lax.fori_loop(0, CELLS // LANES, place, 0, unroll=4)
    for move in moves[0] + moves[1] + moves[2] + [back, whole(0, send1, recv1), whole(1, send2, recv2)]:
        move.wait_send()


TILE = 5


def per_device(zvecs, counts, adjacency, mat_id, shear, ratio, owner_map):
    smem = pl.BlockSpec(memory_space=pltpu.SMEM)
    vmem = pl.BlockSpec(memory_space=pltpu.VMEM)
    rows = pl.pallas_call(
        kernel,
        out_shape=jax.ShapeDtypeStruct((7, 2, CELLS), F32),
        in_specs=[pl.BlockSpec(memory_space=pl.ANY), smem, smem, smem, smem, smem, vmem],
        out_specs=vmem,
        scratch_shapes=[
            pltpu.VMEM((3, ROWS, CELLS + 2 * SLAB), BF16),
            pltpu.VMEM((SLAB, 3 * SLAB), BF16),
            pltpu.VMEM((8 * SLAB, 3 * LANES), BF16),
            pltpu.VMEM((3, 3, ROWS, SLAB), BF16),
            pltpu.VMEM((2, 3, ROWS, SLAB), BF16),
            pltpu.VMEM((2, 3, NV, SLAB), BF16),
            pltpu.VMEM((3, NV, SLAB), BF16),
            pltpu.VMEM((NV // 2, LANES), F32),
            pltpu.VMEM((NV // 2, LANES), F32),
            pltpu.VMEM((PEERS * 8, LANES), F32),
            pltpu.VMEM((PEERS * 8, LANES), F32),
            pltpu.VMEM((PEERS * 8, LANES), F32),
            pltpu.VMEM((PEERS * 8, LANES), F32),
            pltpu.SemaphoreType.DMA((3, 2)),
            pltpu.SemaphoreType.DMA((3, 3)),
            pltpu.SemaphoreType.DMA((3, 3)),
            pltpu.SemaphoreType.DMA((2,)),
            pltpu.SemaphoreType.DMA((2,)),
            pltpu.SemaphoreType.DMA((2,)),
            pltpu.SemaphoreType.REGULAR((2,)),
        ],
        compiler_params=pltpu.CompilerParams(collective_id=0, has_side_effects=True),
        name="assemble",
    )(zvecs, counts, adjacency, mat_id, shear, ratio, owner_map)
    return jnp.transpose(rows, (1, 0, 2))[None]


def solution(mesh):
    placed = (
        P(("gx", "gy", "gz"), None, None, None),
        P(("gx", "gy", "gz")),
        P(("gx", "gy", "gz"), None),
        P(),
        P(),
        P(),
        P(("gx", "gy"), None),
    )
    return jax.shard_map(
        per_device,
        mesh=mesh,
        in_specs=placed,
        out_specs=P(("gx", "gy"), "gz", None, None),
        check_vma=False,
    )
```

```python
import functools

import jax
import jax.numpy as jnp
from jax import lax
from jax.experimental import pallas as pl
from jax.experimental.pallas import tpu as pltpu
from jax.sharding import PartitionSpec as P

BX = 16
SLAB = 256
CELLS = 4096
NV = 64
ROWS = 128
PEERS = 64
LANES = 128
GROUP = 4
UNROLL = 1
UNROLL_POST = 1
MESH = pl.DeviceIdType.MESH
F32 = jnp.float32
BF16 = jnp.bfloat16
TRANS = (((1,), (1,)), ((), ()))


def iota(shape, dim):
    return lax.broadcasted_iota(jnp.int32, shape, dim)


def picked(flag):
    return jnp.where(flag, 1.0, 0.0).astype(BF16)


def by_sub(first, second, shape):
    return jnp.where(iota(shape, len(shape) - 1) < NV, first, second)


def kernel(
    zvecs, counts, adjacency, mat_id, shear, ratio, owner,
    out,
    u, weave, select, near, far, near_y, far_y, back_out, back_in, send1, recv1, send2, recv2,
    load_sem, face_send, face_recv, back_sem, a2a_send, a2a_recv, ring_sem,
):
    gx, gy, gz = lax.axis_index("gx"), lax.axis_index("gy"), lax.axis_index("gz")
    device = (gx * 2 + gy) * PEERS + gz

    barrier = pltpu.get_barrier_semaphore()
    pl.semaphore_signal(barrier, inc=1, device_id={"gx": 1 - gx}, device_id_type=MESH)
    pl.semaphore_signal(barrier, inc=1, device_id={"gy": 1 - gy}, device_id_type=MESH)

    plane, spot = gz // 8, gz & 7
    after, before = (gz + 1) & (PEERS - 1), (gz + PEERS - 1) & (PEERS - 1)
    above, below = (gz + 8) & (PEERS - 1), (gz + PEERS - 8) & (PEERS - 1)
    for peer in [after, before, above, below] + [plane * 8 + (spot ^ k) for k in range(1, 8)]:
        pl.semaphore_signal(barrier, inc=1, device_id={"gz": peer}, device_id_type=MESH)

    loads = []
    for c in range(3):
        for s in range(2):
            loads.append(
                pltpu.make_async_copy(
                    zvecs.at[s, c],
                    u.at[c, pl.ds(s * NV, NV), pl.ds(SLAB, CELLS)],
                    load_sem.at[c, s],
                )
            )
            loads[-1].start()

    def pass_on(step):
        if step > 0:
            pl.semaphore_wait(ring_sem.at[0], 1)
        if step < 4:
            pl.semaphore_signal(
                ring_sem.at[0], inc=1, device_id={"gz": above}, device_id_type=MESH
            )
        if 0 < step < 4:
            pl.semaphore_wait(ring_sem.at[1], 1)
        if step < 3:
            pl.semaphore_signal(
                ring_sem.at[1], inc=1, device_id={"gz": below}, device_id_type=MESH
            )

    inner = iota((SLAB, LANES), 1) % BX
    cell = iota((SLAB, LANES), 0)
    patterns = [
        picked(cell == target)
        for target in ((1 - gy) * 15 * BX + inner, inner * BX + 15, inner * BX)
    ]
    lane_slab = iota((1, LANES), 1) // BX
    for k in range(8):
        part = picked(lane_slab == k)
        for f in range(3):
            select[k * SLAB : (k + 1) * SLAB, f * LANES : (f + 1) * LANES] = patterns[f] * part

    rows_of = iota((ROWS, 1), 0)
    used = jnp.where(rows_of < NV, counts[0], counts[1] + NV)
    keep = jnp.where(rows_of < used, 1.0, 0.0)

    swapped = jnp.full((1, SLAB), adjacency[0, 3 - gy] & 1, jnp.int32)
    keep_last = (swapped + (1 - gy)) > 0

    def layers(c, first, last):
        halves = [u[c, :, SLAB + h * 2048 : SLAB + (h + 1) * 2048] for h in range(2)]
        got = jnp.dot(
            jnp.concatenate(halves, axis=0),
            select[:, first * LANES : last * LANES],
            preferred_element_type=F32,
        )
        return [
            jnp.concatenate(
                [got[h * ROWS : (h + 1) * ROWS, f * LANES : (f + 1) * LANES] * keep for h in range(2)],
                axis=1,
            )
            for f in range(last - first)
        ]

    def send(slot, c, source, landing, target):
        move = pltpu.make_async_remote_copy(
            src_ref=source,
            dst_ref=landing,
            send_sem=face_send.at[slot, c],
            recv_sem=face_recv.at[slot, c],
            device_id=target,
            device_id_type=MESH,
        )
        move.start()
        moves[slot].append(move)

    zero_slab = jnp.zeros((ROWS, SLAB), BF16)
    near_x = (1 - gx) * 15 + 1
    moves = [[], [], []]
    for c in range(3):
        u[c, :, 0:SLAB] = zero_slab
        u[c, :, SLAB + CELLS : 2 * SLAB + CELLS] = zero_slab
        loads[2 * c].wait()
        loads[2 * c + 1].wait()
        layer_y, layer_z, layer_low = layers(c, 0, 3)
        near[1, c] = layer_low.astype(BF16)
        near_y[0, c] = jnp.where(keep_last, layer_y[NV:ROWS], layer_y[0:NV]).astype(BF16)
        near_y[1, c] = jnp.where(keep_last, layer_y[0:NV], layer_y[NV:ROWS]).astype(BF16)
        near[2, c] = layer_z.astype(BF16)
        edge = u[c, :, pl.ds(pl.multiple_of(near_x * SLAB, SLAB), SLAB)].astype(F32)
        near[0, c] = (edge * keep).astype(BF16)
        if c == 0:
            pl.semaphore_wait(barrier, 13)
            pass_on(0)
        send(1, c, near_y.at[1, c], far_y.at[c], {"gy": 1 - gy})
    for c in range(3):
        send(2, c, near.at[2, c], far.at[1, c], {"gz": after})
    for c in range(3):
        send(0, c, near.at[0, c], far.at[0, c], {"gx": 1 - gx})

    row = iota((SLAB, SLAB), 0)
    cell = iota((SLAB, SLAB), 1)
    zpos = cell % BX
    diag = jnp.where(row == cell, 2.0, 0.0)
    along_y = diag - jnp.where((row == cell + BX) | (row == cell - BX), 1.0, 0.0)
    along_z = diag - jnp.where(
        ((row == cell + 1) & (zpos < BX - 1)) | ((row == cell - 1) & (zpos > 0)), 1.0, 0.0
    )
    weave[:, 0:SLAB] = (along_y + along_z).astype(BF16)
    weave[:, 3 * SLAB : 4 * SLAB] = (along_y + along_z + diag).astype(BF16)
    weave[:, SLAB : 2 * SLAB] = along_y.astype(BF16)
    weave[:, 2 * SLAB : 3 * SLAB] = along_z.astype(BF16)

    own = [mat_id[device * 2 + s] for s in range(2)]
    own_shear = [shear[m] for m in own]
    own_ratio = [ratio[m] for m in own]
    by_row = rows_of < NV
    scale = jnp.where(by_row, own_shear[0], own_shear[1])
    extra = jnp.where(by_row, own_shear[0] * own_ratio[0], own_shear[1] * own_ratio[1])

    both = scale + extra

    def stencil(c, total):
        first = 0 if c == 0 else 3 * SLAB

        def group(g, total):
            start = g * (GROUP * SLAB)
            slabs = [u[c, :, start + i * SLAB : start + (i + 1) * SLAB] for i in range(GROUP + 2)]
            stacked = jnp.concatenate(slabs[1:-1], axis=0)
            flat = jnp.dot(stacked, weave[:, first : first + SLAB], preferred_element_type=F32)
            if c > 0:
                lone = jnp.dot(
                    stacked, weave[:, c * SLAB : (c + 1) * SLAB], preferred_element_type=F32
                )
            for i in range(GROUP):
                lower, here, upper = [slabs[i + k].astype(F32) for k in range(3)]
                rest = flat[i * ROWS : (i + 1) * ROWS]
                if c == 0:
                    applied = both * (2.0 * here - (lower + upper)) + scale * rest
                else:
                    lone_part = lone[i * ROWS : (i + 1) * ROWS]
                    applied = scale * (rest - (lower + upper)) + extra * lone_part
                total = total + lax.dot_general(
                    slabs[i + 1], applied.astype(BF16), TRANS, preferred_element_type=F32
                )
            return total

        for g in range(BX // GROUP):
            total = group(g, total)
        return total

    shape = (NV, LANES)

    def couple(left, right, weights):
        result = None
        for c in range(3):
            full = lax.dot_general(left(c), right(c), TRANS, preferred_element_type=F32)
            result = weights[c] * full if result is None else result + weights[c] * full
        return result

    def matched(full, swap):
        turned = pltpu.roll(full, NV, 1)
        return by_sub(
            jnp.where(swap[0], turned[0:NV], full[0:NV]),
            jnp.where(swap[1], turned[NV:ROWS], full[NV:ROWS]),
            shape,
        )

    def pairing(slot, direction):
        swap, values = [], []
        for s in range(2):
            other = adjacency[s, slot]
            there = mat_id[jnp.maximum(other, 0)]
            there_shear, there_ratio = shear[there], ratio[there]
            other = jnp.full((1, LANES), other, jnp.int32)
            swap.append((other >= 0) & ((other & 1) != s))
            valid = jnp.where(other >= 0, -1.0, 0.0)
            line = []
            for c in range(3):
                unit = 1.0 if c == direction else 0.0
                product = (own_shear[s] * (1.0 + own_ratio[s] * unit)) * (
                    there_shear * (1.0 + there_ratio * unit)
                )
                line.append(valid * jnp.sqrt(jnp.full((1, LANES), product, F32)))
            values.append(line)
        return swap, values

    pass_on(1)
    total = stencil(0, jnp.zeros((ROWS, ROWS), F32))
    pass_on(2)
    total = stencil(1, total)
    pass_on(3)

    total = stencil(2, total)
    v_of = iota(shape, 0)
    w_of = iota(shape, 1)
    limit = by_sub(counts[0], counts[1], shape)
    inside = (v_of < limit) & (lax.rem(w_of, NV) < limit)
    block = by_sub(total[0:NV], total[NV:ROWS], shape)
    send1[pl.ds(0, NV, stride=8), :] = jnp.where(inside, block, 0.0)

    swap, values = pairing(1 - gx, 0)
    for move in moves[0]:
        move.wait_recv()
    weights = [jnp.where(by_row, values[0][c], values[1][c]) for c in range(3)]
    full = couple(lambda c: near[0, c], lambda c: far[0, c], weights)
    send1[pl.ds(1, NV, stride=8), :] = matched(full, swap)

    _, values = pairing(3 - gy, 1)
    keep_here = keep_last[:, 0:LANES]
    weights = [jnp.where(keep_here, values[1][c], values[0][c]) for c in range(3)]
    for move in moves[1]:
        move.wait_recv()
    twice = lambda ref, c: jnp.concatenate([ref[c], ref[c]], axis=0)
    kept = couple(lambda c: near_y[0, c], lambda c: twice(far_y, c), weights)
    other = couple(lambda c: far_y[c], lambda c: twice(near_y.at[0], c), weights)
    back_out[...] = by_sub(other[0 : NV // 2], other[NV // 2 : NV], (NV // 2, LANES))
    back = pltpu.make_async_remote_copy(
        src_ref=back_out,
        dst_ref=back_in,
        send_sem=back_sem.at[0],
        recv_sem=back_sem.at[1],
        device_id={"gy": 1 - gy},
        device_id_type=MESH,
    )
    back.start()

    swap, values = pairing(4, 2)
    for move in moves[2]:
        move.wait_recv()
    weights = [jnp.where(by_row, values[0][c], values[1][c]) for c in range(3)]
    full = couple(lambda c: near[1, c], lambda c: far[1, c], weights)
    send1[pl.ds(3, NV, stride=8), :] = matched(full, swap)
    weights = [by_sub(values[0][c], values[1][c], (1, LANES)) for c in range(3)]
    full = couple(lambda c: far[1, c], lambda c: near[1, c], weights)
    send1[pl.ds(4, NV, stride=8), :] = matched(full, swap)

    back.wait_recv()
    packed = back_in[...]
    turned = pltpu.roll(packed, NV, 1)
    given = jnp.concatenate(
        [by_sub(packed, turned, packed.shape), by_sub(turned, packed, packed.shape)], axis=0
    )
    send1[pl.ds(2, NV, stride=8), :] = by_sub(
        jnp.where(keep_here, given, kept), jnp.where(keep_here, kept, given), shape
    )

    def exchange(phase, source, target):
        def post(k, carry):
            ring = k >> 3
            step = (ring + 1) >> 1
            ring = 4 + step * (2 * (ring & 1) - 1)
            peer = (((plane + ring) & 7) << 3) + ((gz + k + 1) & 7)
            pltpu.make_async_remote_copy(
                src_ref=source.at[pl.ds(pl.multiple_of(peer * 8, 8), TILE)],
                dst_ref=target.at[pl.ds(pl.multiple_of(gz * 8, 8), TILE)],
                send_sem=a2a_send.at[phase],
                recv_sem=a2a_recv.at[phase],
                device_id={"gz": peer},
                device_id_type=MESH,
            ).start()
            return carry

        lax.fori_loop(0, PEERS - 1, post, 0, unroll=UNROLL_POST)
        mine = pl.ds(pl.multiple_of(gz * 8, 8), 8)
        target[mine, :] = source[mine, :]

    def whole(phase, source, target):
        size = (PEERS - 1) * TILE
        return pltpu.make_async_remote_copy(
            src_ref=source.at[pl.ds(0, size)],
            dst_ref=target.at[pl.ds(0, size)],
            send_sem=a2a_send.at[phase],
            recv_sem=a2a_recv.at[phase],
            device_id={"gz": after},
            device_id_type=MESH,
        )

    pass_on(4)
    exchange(0, send1, recv1)

    line = iota((ROWS, ROWS), 0)
    spot = iota((ROWS, ROWS), 1)
    half = spot // NV
    holder = lax.rem(spot, NV)
    places = owner[...].astype(F32).astype(BF16)
    places = jnp.broadcast_to(places, (8, ROWS))
    want = (2 * lax.rem(line, NV) + line // NV).astype(F32)

    def moved(shift):
        sub = 2 * lax.rem(holder + (PEERS - shift), PEERS) + half
        place = jnp.dot(places, picked(line == sub), preferred_element_type=F32)
        hit = picked(place[0:1, :] == want)
        return jnp.concatenate([hit, hit, hit], axis=1)

    straight, shifted = moved(0), moved(1)
    whole(0, send1, recv1).wait_recv()
    for b in range(5):
        chunk = recv1[pl.ds(b, PEERS, stride=8), :]
        turned = pltpu.roll(chunk, NV, 1)
        chunk = jnp.concatenate(
            [by_sub(chunk, turned, shape), by_sub(turned, chunk, shape)], axis=0
        )
        high = chunk.astype(BF16)
        left = chunk - high.astype(F32)
        middle = left.astype(BF16)
        low = (left - middle.astype(F32)).astype(BF16)
        full = jnp.dot(
            shifted if b == 4 else straight,
            jnp.concatenate([high, middle, low], axis=0),
            preferred_element_type=F32,
        )
        send2[pl.ds(b, PEERS, stride=8), :] = by_sub(full[0:NV], full[NV:ROWS], shape)

    exchange(1, send2, recv2)
    tile = (8, LANES)
    b_of = iota(tile, 0)
    x_at, y_at = 2 - gx, 4 - gy
    plain = (b_of == 0) | ((b_of == x_at) & (gx == 1))
    once = ((b_of == x_at) & (gx == 0)) | ((b_of == y_at) & (gy == 1))
    twice = ((b_of == y_at) & (gy == 0)) | (b_of > 4)
    whole(1, send2, recv2).wait_recv()

    def place(m, carry):
        pair = [recv2[pl.ds(pl.multiple_of((2 * m + i) * 8, 8), 8), :] for i in range(2)]
        turned = [pltpu.roll(t, NV, 1) for t in pair]
        for p, value in enumerate(
            (by_sub(pair[0], turned[1], tile), by_sub(turned[0], pair[1], tile))
        ):
            value = jnp.where(
                plain,
                value,
                jnp.where(
                    once,
                    pltpu.roll(value, 1, 0),
                    jnp.where(twice, pltpu.roll(value, 2, 0), 0.0),
                ),
            )
            out[:, p, pl.ds(pl.multiple_of(m * LANES, LANES), LANES)] = value[0:7]
        return carry

    lax.fori_loop(0, CELLS // LANES, place, 0, unroll=4)
    for move in moves[0] + moves[1] + moves[2] + [back, whole(0, send1, recv1), whole(1, send2, recv2)]:
        move.wait_send()


TILE = 5


def per_device(zvecs, counts, adjacency, mat_id, shear, ratio, owner_map):
    smem = pl.BlockSpec(memory_space=pltpu.SMEM)
    vmem = pl.BlockSpec(memory_space=pltpu.VMEM)
    rows = pl.pallas_call(
        kernel,
        out_shape=jax.ShapeDtypeStruct((7, 2, CELLS), F32),
        in_specs=[pl.BlockSpec(memory_space=pl.ANY), smem, smem, smem, smem, smem, vmem],
        out_specs=vmem,
        scratch_shapes=[
            pltpu.VMEM((3, ROWS, CELLS + 2 * SLAB), BF16),
            pltpu.VMEM((SLAB, 4 * SLAB), BF16),
            pltpu.VMEM((8 * SLAB, 3 * LANES), BF16),
            pltpu.VMEM((3, 3, ROWS, SLAB), BF16),
            pltpu.VMEM((2, 3, ROWS, SLAB), BF16),
            pltpu.VMEM((2, 3, NV, SLAB), BF16),
            pltpu.VMEM((3, NV, SLAB), BF16),
            pltpu.VMEM((NV // 2, LANES), F32),
            pltpu.VMEM((NV // 2, LANES), F32),
            pltpu.VMEM((PEERS * 8, LANES), F32),
            pltpu.VMEM((PEERS * 8, LANES), F32),
            pltpu.VMEM((PEERS * 8, LANES), F32),
            pltpu.VMEM((PEERS * 8, LANES), F32),
            pltpu.SemaphoreType.DMA((3, 2)),
            pltpu.SemaphoreType.DMA((3, 3)),
            pltpu.SemaphoreType.DMA((3, 3)),
            pltpu.SemaphoreType.DMA((2,)),
            pltpu.SemaphoreType.DMA((2,)),
            pltpu.SemaphoreType.DMA((2,)),
            pltpu.SemaphoreType.REGULAR((2,)),
        ],
        compiler_params=pltpu.CompilerParams(collective_id=0, has_side_effects=True),
        name="assemble",
    )(zvecs, counts, adjacency, mat_id, shear, ratio, owner_map)
    return jnp.transpose(rows, (1, 0, 2))[None]


def solution(mesh):
    placed = (
        P(("gx", "gy", "gz"), None, None, None),
        P(("gx", "gy", "gz")),
        P(("gx", "gy", "gz"), None),
        P(),
        P(),
        P(),
        P(("gx", "gy"), None),
    )
    return jax.shard_map(
        per_device,
        mesh=mesh,
        in_specs=placed,
        out_specs=P(("gx", "gy"), "gz", None, None),
        check_vma=False,
    )
```

```python
import functools

import jax
import jax.numpy as jnp
from jax import lax
from jax.experimental import pallas as pl
from jax.experimental.pallas import tpu as pltpu
from jax.sharding import PartitionSpec as P

BX = 16
SLAB = 256
CELLS = 4096
NV = 64
ROWS = 128
PEERS = 64
LANES = 128
GROUP = 4
UNROLL = 1
UNROLL_POST = 1
MESH = pl.DeviceIdType.MESH
F32 = jnp.float32
BF16 = jnp.bfloat16
TRANS = (((1,), (1,)), ((), ()))


def iota(shape, dim):
    return lax.broadcasted_iota(jnp.int32, shape, dim)


def picked(flag):
    return jnp.where(flag, 1.0, 0.0).astype(BF16)


def by_sub(first, second, shape):
    return jnp.where(iota(shape, len(shape) - 1) < NV, first, second)


def kernel(
    zvecs, counts, adjacency, mat_id, shear, ratio, owner,
    out,
    u, weave, select, near, far, near_y, far_y, back_out, back_in, send1, recv1, send2, recv2,
    load_sem, face_send, face_recv, back_sem, a2a_send, a2a_recv, ring_sem,
):
    gx, gy, gz = lax.axis_index("gx"), lax.axis_index("gy"), lax.axis_index("gz")
    device = (gx * 2 + gy) * PEERS + gz

    barrier = pltpu.get_barrier_semaphore()
    pl.semaphore_signal(barrier, inc=1, device_id={"gx": 1 - gx}, device_id_type=MESH)
    pl.semaphore_signal(barrier, inc=1, device_id={"gy": 1 - gy}, device_id_type=MESH)

    plane, spot = gz // 8, gz & 7
    after, before = (gz + 1) & (PEERS - 1), (gz + PEERS - 1) & (PEERS - 1)
    above, below = (gz + 8) & (PEERS - 1), (gz + PEERS - 8) & (PEERS - 1)
    for peer in [after, before, above, below] + [plane * 8 + (spot ^ k) for k in range(1, 8)]:
        pl.semaphore_signal(barrier, inc=1, device_id={"gz": peer}, device_id_type=MESH)

    loads = []
    for c in range(3):
        for s in range(2):
            loads.append(
                pltpu.make_async_copy(
                    zvecs.at[s, c],
                    u.at[c, pl.ds(s * NV, NV), pl.ds(SLAB, CELLS)],
                    load_sem.at[c, s],
                )
            )
            loads[-1].start()

    def pass_on(step):
        if step > 0:
            pl.semaphore_wait(ring_sem.at[0], 1)
        if step < 4:
            pl.semaphore_signal(
                ring_sem.at[0], inc=1, device_id={"gz": above}, device_id_type=MESH
            )
        if 0 < step < 4:
            pl.semaphore_wait(ring_sem.at[1], 1)
        if step < 3:
            pl.semaphore_signal(
                ring_sem.at[1], inc=1, device_id={"gz": below}, device_id_type=MESH
            )

    inner = iota((SLAB, LANES), 1) % BX
    cell = iota((SLAB, LANES), 0)
    patterns = [
        picked(cell == target)
        for target in ((1 - gy) * 15 * BX + inner, inner * BX + 15, inner * BX)
    ]
    lane_slab = iota((1, LANES), 1) // BX
    for k in range(8):
        part = picked(lane_slab == k)
        for f in range(3):
            select[k * SLAB : (k + 1) * SLAB, f * LANES : (f + 1) * LANES] = patterns[f] * part

    rows_of = iota((ROWS, 1), 0)
    used = jnp.where(rows_of < NV, counts[0], counts[1] + NV)
    keep = jnp.where(rows_of < used, 1.0, 0.0)

    swapped = jnp.full((1, SLAB), adjacency[0, 3 - gy] & 1, jnp.int32)
    keep_last = (swapped + (1 - gy)) > 0

    def layers(c, first, last):
        halves = [u[c, :, SLAB + h * 2048 : SLAB + (h + 1) * 2048] for h in range(2)]
        got = jnp.dot(
            jnp.concatenate(halves, axis=0),
            select[:, first * LANES : last * LANES],
            preferred_element_type=F32,
        )
        return [
            jnp.concatenate(
                [got[h * ROWS : (h + 1) * ROWS, f * LANES : (f + 1) * LANES] * keep for h in range(2)],
                axis=1,
            )
            for f in range(last - first)
        ]

    def send(slot, c, source, landing, target):
        move = pltpu.make_async_remote_copy(
            src_ref=source,
            dst_ref=landing,
            send_sem=face_send.at[slot, c],
            recv_sem=face_recv.at[slot, c],
            device_id=target,
            device_id_type=MESH,
        )
        move.start()
        moves[slot].append(move)

    zero_slab = jnp.zeros((ROWS, SLAB), BF16)
    near_x = (1 - gx) * 15 + 1
    moves = [[], [], []]
    for c in range(3):
        u[c, :, 0:SLAB] = zero_slab
        u[c, :, SLAB + CELLS : 2 * SLAB + CELLS] = zero_slab
        loads[2 * c].wait()
        loads[2 * c + 1].wait()
        layer_y, layer_z, layer_low = layers(c, 0, 3)
        near[1, c] = layer_low.astype(BF16)
        near_y[0, c] = jnp.where(keep_last, layer_y[NV:ROWS], layer_y[0:NV]).astype(BF16)
        near_y[1, c] = jnp.where(keep_last, layer_y[0:NV], layer_y[NV:ROWS]).astype(BF16)
        near[2, c] = layer_z.astype(BF16)
        edge = u[c, :, pl.ds(pl.multiple_of(near_x * SLAB, SLAB), SLAB)].astype(F32)
        near[0, c] = (edge * keep).astype(BF16)
        if c == 0:
            pl.semaphore_wait(barrier, 13)
            pass_on(0)
        send(1, c, near_y.at[1, c], far_y.at[c], {"gy": 1 - gy})
    for c in range(3):
        send(2, c, near.at[2, c], far.at[1, c], {"gz": after})
    for c in range(3):
        send(0, c, near.at[0, c], far.at[0, c], {"gx": 1 - gx})

    row = iota((SLAB, SLAB), 0)
    cell = iota((SLAB, SLAB), 1)
    zpos = cell % BX
    diag = jnp.where(row == cell, 2.0, 0.0)
    along_y = diag - jnp.where((row == cell + BX) | (row == cell - BX), 1.0, 0.0)
    along_z = diag - jnp.where(
        ((row == cell + 1) & (zpos < BX - 1)) | ((row == cell - 1) & (zpos > 0)), 1.0, 0.0
    )
    weave[:, 0:SLAB] = (along_y + along_z).astype(BF16)
    weave[:, 3 * SLAB : 4 * SLAB] = (along_y + along_z + diag).astype(BF16)
    weave[:, SLAB : 2 * SLAB] = along_y.astype(BF16)
    weave[:, 2 * SLAB : 3 * SLAB] = along_z.astype(BF16)

    own = [mat_id[device * 2 + s] for s in range(2)]
    own_shear = [shear[m] for m in own]
    own_ratio = [ratio[m] for m in own]
    by_row = rows_of < NV
    scale = jnp.where(by_row, own_shear[0], own_shear[1])
    extra = jnp.where(by_row, own_shear[0] * own_ratio[0], own_shear[1] * own_ratio[1])

    both = scale + extra

    def stencil(c, total):
        first = 0 if c == 0 else 3 * SLAB

        def group(g, total):
            start = g * (GROUP * SLAB)
            slabs = [u[c, :, start + i * SLAB : start + (i + 1) * SLAB] for i in range(GROUP + 2)]
            stacked = jnp.concatenate(slabs[1:-1], axis=0)
            flat = jnp.dot(stacked, weave[:, first : first + SLAB], preferred_element_type=F32)
            if c > 0:
                lone = jnp.dot(
                    stacked, weave[:, c * SLAB : (c + 1) * SLAB], preferred_element_type=F32
                )
            for i in range(GROUP):
                lower, here, upper = [slabs[i + k].astype(F32) for k in range(3)]
                rest = flat[i * ROWS : (i + 1) * ROWS]
                if c == 0:
                    applied = both * (2.0 * here - (lower + upper)) + scale * rest
                else:
                    lone_part = lone[i * ROWS : (i + 1) * ROWS]
                    applied = scale * (rest - (lower + upper)) + extra * lone_part
                total = total + lax.dot_general(
                    slabs[i + 1], applied.astype(BF16), TRANS, preferred_element_type=F32
                )
            return total

        for g in range(BX // GROUP):
            total = group(g, total)
        return total

    shape = (NV, LANES)

    def couple(left, right, weights):
        result = None
        for c in range(3):
            full = lax.dot_general(left(c), right(c), TRANS, preferred_element_type=F32)
            result = weights[c] * full if result is None else result + weights[c] * full
        return result

    def matched(full, swap):
        turned = pltpu.roll(full, NV, 1)
        return by_sub(
            jnp.where(swap[0], turned[0:NV], full[0:NV]),
            jnp.where(swap[1], turned[NV:ROWS], full[NV:ROWS]),
            shape,
        )

    def pairing(slot, direction):
        swap, values = [], []
        for s in range(2):
            other = adjacency[s, slot]
            there = mat_id[jnp.maximum(other, 0)]
            there_shear, there_ratio = shear[there], ratio[there]
            other = jnp.full((1, LANES), other, jnp.int32)
            swap.append((other >= 0) & ((other & 1) != s))
            valid = jnp.where(other >= 0, -1.0, 0.0)
            line = []
            for c in range(3):
                unit = 1.0 if c == direction else 0.0
                product = (own_shear[s] * (1.0 + own_ratio[s] * unit)) * (
                    there_shear * (1.0 + there_ratio * unit)
                )
                line.append(valid * jnp.sqrt(jnp.full((1, LANES), product, F32)))
            values.append(line)
        return swap, values

    pass_on(1)
    total = stencil(0, jnp.zeros((ROWS, ROWS), F32))
    pass_on(2)
    total = stencil(1, total)
    pass_on(3)

    total = stencil(2, total)
    v_of = iota(shape, 0)
    w_of = iota(shape, 1)
    limit = by_sub(counts[0], counts[1], shape)
    inside = (v_of < limit) & (lax.rem(w_of, NV) < limit)
    block = by_sub(total[0:NV], total[NV:ROWS], shape)
    send1[pl.ds(0, NV, stride=8), :] = jnp.where(inside, block, 0.0)

    swap, values = pairing(1 - gx, 0)
    for move in moves[0]:
        move.wait_recv()
    weights = [jnp.where(by_row, values[0][c], values[1][c]) for c in range(3)]
    full = couple(lambda c: near[0, c], lambda c: far[0, c], weights)
    send1[pl.ds(1, NV, stride=8), :] = matched(full, swap)

    _, values = pairing(3 - gy, 1)
    keep_here = keep_last[:, 0:LANES]
    weights = [jnp.where(keep_here, values[1][c], values[0][c]) for c in range(3)]
    for move in moves[1]:
        move.wait_recv()
    twice = lambda ref, c: jnp.concatenate([ref[c], ref[c]], axis=0)
    kept = couple(lambda c: near_y[0, c], lambda c: twice(far_y, c), weights)
    other = couple(lambda c: far_y[c], lambda c: twice(near_y.at[0], c), weights)
    back_out[...] = by_sub(other[0 : NV // 2], other[NV // 2 : NV], (NV // 2, LANES))
    back = pltpu.make_async_remote_copy(
        src_ref=back_out,
        dst_ref=back_in,
        send_sem=back_sem.at[0],
        recv_sem=back_sem.at[1],
        device_id={"gy": 1 - gy},
        device_id_type=MESH,
    )
    back.start()

    swap, values = pairing(4, 2)
    for move in moves[2]:
        move.wait_recv()
    weights = [jnp.where(by_row, values[0][c], values[1][c]) for c in range(3)]
    full = couple(lambda c: near[1, c], lambda c: far[1, c], weights)
    send1[pl.ds(3, NV, stride=8), :] = matched(full, swap)
    weights = [by_sub(values[0][c], values[1][c], (1, LANES)) for c in range(3)]
    full = couple(lambda c: far[1, c], lambda c: near[1, c], weights)
    send1[pl.ds(4, NV, stride=8), :] = matched(full, swap)

    back.wait_recv()
    packed = back_in[...]
    turned = pltpu.roll(packed, NV, 1)
    given = jnp.concatenate(
        [by_sub(packed, turned, packed.shape), by_sub(turned, packed, packed.shape)], axis=0
    )
    send1[pl.ds(2, NV, stride=8), :] = by_sub(
        jnp.where(keep_here, given, kept), jnp.where(keep_here, kept, given), shape
    )

    def exchange(phase, source, target):
        def post(k, carry):
            ring = k >> 3
            step = (ring + 1) >> 1
            ring = 4 + step * (2 * (ring & 1) - 1)
            peer = (((plane + ring) & 7) << 3) + ((gz + k + 1) & 7)
            pltpu.make_async_remote_copy(
                src_ref=source.at[pl.ds(pl.multiple_of(peer * 8, 8), TILE)],
                dst_ref=target.at[pl.ds(pl.multiple_of(gz * 8, 8), TILE)],
                send_sem=a2a_send.at[phase],
                recv_sem=a2a_recv.at[phase],
                device_id={"gz": peer},
                device_id_type=MESH,
            ).start()
            return carry

        lax.fori_loop(0, PEERS - 1, post, 0, unroll=UNROLL_POST)
        mine = pl.ds(pl.multiple_of(gz * 8, 8), 8)
        target[mine, :] = source[mine, :]

    def whole(phase, source, target):
        size = (PEERS - 1) * TILE
        return pltpu.make_async_remote_copy(
            src_ref=source.at[pl.ds(0, size)],
            dst_ref=target.at[pl.ds(0, size)],
            send_sem=a2a_send.at[phase],
            recv_sem=a2a_recv.at[phase],
            device_id={"gz": after},
            device_id_type=MESH,
        )

    pass_on(4)
    exchange(0, send1, recv1)

    line = iota((ROWS, ROWS), 0)
    spot = iota((ROWS, ROWS), 1)
    half = spot // NV
    holder = lax.rem(spot, NV)
    places = owner[...].astype(F32).astype(BF16)
    places = jnp.broadcast_to(places, (8, ROWS))
    want = (2 * lax.rem(line, NV) + line // NV).astype(F32)

    def moved(shift):
        sub = 2 * lax.rem(holder + (PEERS - shift), PEERS) + half
        place = jnp.dot(places, picked(line == sub), preferred_element_type=F32)
        hit = picked(place[0:1, :] == want)
        return jnp.concatenate([hit, hit, hit], axis=1)

    straight, shifted = moved(0), moved(1)
    whole(0, send1, recv1).wait_recv()
    for b in range(5):
        chunk = recv1[pl.ds(b, PEERS, stride=8), :]
        turned = pltpu.roll(chunk, NV, 1)
        chunk = jnp.concatenate(
            [by_sub(chunk, turned, shape), by_sub(turned, chunk, shape)], axis=0
        )
        high = chunk.astype(BF16)
        left = chunk - high.astype(F32)
        middle = left.astype(BF16)
        low = (left - middle.astype(F32)).astype(BF16)
        full = jnp.dot(
            shifted if b == 4 else straight,
            jnp.concatenate([high, middle, low], axis=0),
            preferred_element_type=F32,
        )
        send2[pl.ds(b, PEERS, stride=8), :] = by_sub(full[0:NV], full[NV:ROWS], shape)

    exchange(1, send2, recv2)
    whole(1, send2, recv2).wait_recv()
    out[...] = recv2[...]
    for move in moves[0] + moves[1] + moves[2] + [back, whole(0, send1, recv1), whole(1, send2, recv2)]:
        move.wait_send()


def lay_out(recv2, out):
    gx, gy = lax.axis_index("gx"), lax.axis_index("gy")
    tile = (8, LANES)
    b_of = iota(tile, 0)
    x_at, y_at = 2 - gx, 4 - gy
    plain = (b_of == 0) | ((b_of == x_at) & (gx == 1))
    once = ((b_of == x_at) & (gx == 0)) | ((b_of == y_at) & (gy == 1))
    twice = ((b_of == y_at) & (gy == 0)) | (b_of > 4)
    def place(m, carry):
        pair = [recv2[pl.ds(pl.multiple_of((2 * m + i) * 8, 8), 8), :] for i in range(2)]
        turned = [pltpu.roll(t, NV, 1) for t in pair]
        for p, value in enumerate(
            (by_sub(pair[0], turned[1], tile), by_sub(turned[0], pair[1], tile))
        ):
            value = jnp.where(
                plain,
                value,
                jnp.where(
                    once,
                    pltpu.roll(value, 1, 0),
                    jnp.where(twice, pltpu.roll(value, 2, 0), 0.0),
                ),
            )
            out[:, p, pl.ds(pl.multiple_of(m * LANES, LANES), LANES)] = value[0:7]
        return carry

    lax.fori_loop(0, CELLS // LANES, place, 0, unroll=4)


TILE = 5


def per_device(zvecs, counts, adjacency, mat_id, shear, ratio, owner_map):
    smem = pl.BlockSpec(memory_space=pltpu.SMEM)
    vmem = pl.BlockSpec(memory_space=pltpu.VMEM)
    rows = pl.pallas_call(
        kernel,
        out_shape=pltpu.VMEM((PEERS * 8, LANES), F32),
        in_specs=[pl.BlockSpec(memory_space=pl.ANY), smem, smem, smem, smem, smem, vmem],
        out_specs=vmem,
        scratch_shapes=[
            pltpu.VMEM((3, ROWS, CELLS + 2 * SLAB), BF16),
            pltpu.VMEM((SLAB, 4 * SLAB), BF16),
            pltpu.VMEM((8 * SLAB, 3 * LANES), BF16),
            pltpu.VMEM((3, 3, ROWS, SLAB), BF16),
            pltpu.VMEM((2, 3, ROWS, SLAB), BF16),
            pltpu.VMEM((2, 3, NV, SLAB), BF16),
            pltpu.VMEM((3, NV, SLAB), BF16),
            pltpu.VMEM((NV // 2, LANES), F32),
            pltpu.VMEM((NV // 2, LANES), F32),
            pltpu.VMEM((PEERS * 8, LANES), F32),
            pltpu.VMEM((PEERS * 8, LANES), F32),
            pltpu.VMEM((PEERS * 8, LANES), F32),
            pltpu.VMEM((PEERS * 8, LANES), F32),
            pltpu.SemaphoreType.DMA((3, 2)),
            pltpu.SemaphoreType.DMA((3, 3)),
            pltpu.SemaphoreType.DMA((3, 3)),
            pltpu.SemaphoreType.DMA((2,)),
            pltpu.SemaphoreType.DMA((2,)),
            pltpu.SemaphoreType.DMA((2,)),
            pltpu.SemaphoreType.REGULAR((2,)),
        ],
        compiler_params=pltpu.CompilerParams(collective_id=0, has_side_effects=True),
        name="assemble",
    )(zvecs, counts, adjacency, mat_id, shear, ratio, owner_map)
    rows = pl.pallas_call(
        lay_out,
        out_shape=jax.ShapeDtypeStruct((7, 2, CELLS), F32),
        in_specs=[vmem],
        out_specs=vmem,
        name="lay_out",
    )(pltpu.with_memory_space_constraint(rows, pltpu.VMEM))
    return jnp.transpose(rows, (1, 0, 2))[None]


def solution(mesh):
    placed = (
        P(("gx", "gy", "gz"), None, None, None),
        P(("gx", "gy", "gz")),
        P(("gx", "gy", "gz"), None),
        P(),
        P(),
        P(),
        P(("gx", "gy"), None),
    )
    return jax.shard_map(
        per_device,
        mesh=mesh,
        in_specs=placed,
        out_specs=P(("gx", "gy"), "gz", None, None),
        check_vma=False,
    )
```

```python
import functools

import jax
import jax.numpy as jnp
from jax import lax
from jax.experimental import pallas as pl
from jax.experimental.pallas import tpu as pltpu
from jax.sharding import PartitionSpec as P

BX = 16
SLAB = 256
CELLS = 4096
NV = 64
ROWS = 128
PEERS = 64
LANES = 128
GROUP = 4
UNROLL = 1
UNROLL_POST = 1
MESH = pl.DeviceIdType.MESH
F32 = jnp.float32
BF16 = jnp.bfloat16
TRANS = (((1,), (1,)), ((), ()))


def iota(shape, dim):
    return lax.broadcasted_iota(jnp.int32, shape, dim)


def picked(flag):
    return jnp.where(flag, 1.0, 0.0).astype(BF16)


def by_sub(first, second, shape):
    return jnp.where(iota(shape, len(shape) - 1) < NV, first, second)


def kernel(
    zvecs, counts, adjacency, mat_id, shear, ratio, owner,
    out,
    u, weave, select, near, far, near_y, far_y, back_out, back_in, send1, recv1, send2, recv2,
    load_sem, face_send, face_recv, back_sem, a2a_send, a2a_recv, ring_sem,
):
    gx, gy, gz = lax.axis_index("gx"), lax.axis_index("gy"), lax.axis_index("gz")
    device = (gx * 2 + gy) * PEERS + gz

    barrier = pltpu.get_barrier_semaphore()
    pl.semaphore_signal(barrier, inc=1, device_id={"gx": 1 - gx}, device_id_type=MESH)
    pl.semaphore_signal(barrier, inc=1, device_id={"gy": 1 - gy}, device_id_type=MESH)

    plane, spot = gz // 8, gz & 7
    after, before = (gz + 1) & (PEERS - 1), (gz + PEERS - 1) & (PEERS - 1)
    above, below = (gz + 8) & (PEERS - 1), (gz + PEERS - 8) & (PEERS - 1)
    for peer in [after, before, above, below] + [plane * 8 + (spot ^ k) for k in range(1, 8)]:
        pl.semaphore_signal(barrier, inc=1, device_id={"gz": peer}, device_id_type=MESH)

    loads = []
    for c in range(3):
        for s in range(2):
            loads.append(
                pltpu.make_async_copy(
                    zvecs.at[s, c],
                    u.at[c, pl.ds(s * NV, NV), pl.ds(SLAB, CELLS)],
                    load_sem.at[c, s],
                )
            )
            loads[-1].start()

    def pass_on(step):
        if step > 0:
            pl.semaphore_wait(ring_sem.at[0], 1)
        if step < 4:
            pl.semaphore_signal(
                ring_sem.at[0], inc=1, device_id={"gz": above}, device_id_type=MESH
            )
        if 0 < step < 4:
            pl.semaphore_wait(ring_sem.at[1], 1)
        if step < 3:
            pl.semaphore_signal(
                ring_sem.at[1], inc=1, device_id={"gz": below}, device_id_type=MESH
            )

    inner = iota((SLAB, LANES), 1) % BX
    cell = iota((SLAB, LANES), 0)
    patterns = [
        picked(cell == target)
        for target in ((1 - gy) * 15 * BX + inner, inner * BX + 15, inner * BX)
    ]
    lane_slab = iota((1, LANES), 1) // BX
    for k in range(8):
        part = picked(lane_slab == k)
        for f in range(3):
            select[k * SLAB : (k + 1) * SLAB, f * LANES : (f + 1) * LANES] = patterns[f] * part

    rows_of = iota((ROWS, 1), 0)
    used = jnp.where(rows_of < NV, counts[0], counts[1] + NV)
    keep = jnp.where(rows_of < used, 1.0, 0.0)

    swapped = jnp.full((1, SLAB), adjacency[0, 3 - gy] & 1, jnp.int32)
    keep_last = (swapped + (1 - gy)) > 0

    def layers(c, first, last):
        halves = [u[c, :, SLAB + h * 2048 : SLAB + (h + 1) * 2048] for h in range(2)]
        got = jnp.dot(
            jnp.concatenate(halves, axis=0),
            select[:, first * LANES : last * LANES],
            preferred_element_type=F32,
        )
        return [
            jnp.concatenate(
                [got[h * ROWS : (h + 1) * ROWS, f * LANES : (f + 1) * LANES] * keep for h in range(2)],
                axis=1,
            )
            for f in range(last - first)
        ]

    def send(slot, c, source, landing, target):
        move = pltpu.make_async_remote_copy(
            src_ref=source,
            dst_ref=landing,
            send_sem=face_send.at[slot, c],
            recv_sem=face_recv.at[slot, c],
            device_id=target,
            device_id_type=MESH,
        )
        move.start()
        moves[slot].append(move)

    zero_slab = jnp.zeros((ROWS, SLAB), BF16)
    near_x = (1 - gx) * 15 + 1
    moves = [[], [], []]
    for c in range(3):
        u[c, :, 0:SLAB] = zero_slab
        u[c, :, SLAB + CELLS : 2 * SLAB + CELLS] = zero_slab
        loads[2 * c].wait()
        loads[2 * c + 1].wait()
        layer_y, layer_z = layers(c, 0, 2)
        near_y[0, c] = jnp.where(keep_last, layer_y[NV:ROWS], layer_y[0:NV]).astype(BF16)
        near_y[1, c] = jnp.where(keep_last, layer_y[0:NV], layer_y[NV:ROWS]).astype(BF16)
        near[2, c] = layer_z.astype(BF16)
        edge = u[c, :, pl.ds(pl.multiple_of(near_x * SLAB, SLAB), SLAB)].astype(F32)
        near[0, c] = (edge * keep).astype(BF16)
        if c == 0:
            pl.semaphore_wait(barrier, 13)
            pass_on(0)
        send(1, c, near_y.at[1, c], far_y.at[c], {"gy": 1 - gy})
    for c in range(3):
        send(2, c, near.at[2, c], far.at[1, c], {"gz": after})
    for c in range(3):
        send(0, c, near.at[0, c], far.at[0, c], {"gx": 1 - gx})

    row = iota((SLAB, SLAB), 0)
    cell = iota((SLAB, SLAB), 1)
    zpos = cell % BX
    diag = jnp.where(row == cell, 2.0, 0.0)
    along_y = diag - jnp.where((row == cell + BX) | (row == cell - BX), 1.0, 0.0)
    along_z = diag - jnp.where(
        ((row == cell + 1) & (zpos < BX - 1)) | ((row == cell - 1) & (zpos > 0)), 1.0, 0.0
    )
    weave[:, 0:SLAB] = (along_y + along_z).astype(BF16)
    weave[:, 3 * SLAB : 4 * SLAB] = (along_y + along_z + diag).astype(BF16)
    weave[:, SLAB : 2 * SLAB] = along_y.astype(BF16)
    weave[:, 2 * SLAB : 3 * SLAB] = along_z.astype(BF16)

    own = [mat_id[device * 2 + s] for s in range(2)]
    own_shear = [shear[m] for m in own]
    own_ratio = [ratio[m] for m in own]
    by_row = rows_of < NV
    scale = jnp.where(by_row, own_shear[0], own_shear[1])
    extra = jnp.where(by_row, own_shear[0] * own_ratio[0], own_shear[1] * own_ratio[1])

    both = scale + extra

    def stencil(c, total):
        first = 0 if c == 0 else 3 * SLAB

        def group(g, total):
            start = g * (GROUP * SLAB)
            slabs = [u[c, :, start + i * SLAB : start + (i + 1) * SLAB] for i in range(GROUP + 2)]
            stacked = jnp.concatenate(slabs[1:-1], axis=0)
            flat = jnp.dot(stacked, weave[:, first : first + SLAB], preferred_element_type=F32)
            if c > 0:
                lone = jnp.dot(
                    stacked, weave[:, c * SLAB : (c + 1) * SLAB], preferred_element_type=F32
                )
            for i in range(GROUP):
                lower, here, upper = [slabs[i + k].astype(F32) for k in range(3)]
                rest = flat[i * ROWS : (i + 1) * ROWS]
                if c == 0:
                    applied = both * (2.0 * here - (lower + upper)) + scale * rest
                else:
                    lone_part = lone[i * ROWS : (i + 1) * ROWS]
                    applied = scale * (rest - (lower + upper)) + extra * lone_part
                total = total + lax.dot_general(
                    slabs[i + 1], applied.astype(BF16), TRANS, preferred_element_type=F32
                )
            return total

        for g in range(BX // GROUP):
            total = group(g, total)
        return total

    shape = (NV, LANES)

    def couple(left, right, weights):
        result = None
        for c in range(3):
            full = lax.dot_general(left(c), right(c), TRANS, preferred_element_type=F32)
            result = weights[c] * full if result is None else result + weights[c] * full
        return result

    def matched(full, swap):
        turned = pltpu.roll(full, NV, 1)
        return by_sub(
            jnp.where(swap[0], turned[0:NV], full[0:NV]),
            jnp.where(swap[1], turned[NV:ROWS], full[NV:ROWS]),
            shape,
        )

    def pairing(slot, direction):
        swap, values = [], []
        for s in range(2):
            other = adjacency[s, slot]
            there = mat_id[jnp.maximum(other, 0)]
            there_shear, there_ratio = shear[there], ratio[there]
            other = jnp.full((1, LANES), other, jnp.int32)
            swap.append((other >= 0) & ((other & 1) != s))
            valid = jnp.where(other >= 0, -1.0, 0.0)
            line = []
            for c in range(3):
                unit = 1.0 if c == direction else 0.0
                product = (own_shear[s] * (1.0 + own_ratio[s] * unit)) * (
                    there_shear * (1.0 + there_ratio * unit)
                )
                line.append(valid * jnp.sqrt(jnp.full((1, LANES), product, F32)))
            values.append(line)
        return swap, values

    pass_on(1)
    total = stencil(0, jnp.zeros((ROWS, ROWS), F32))
    for c in range(3):
        near[1, c] = layers(c, 2, 3)[0].astype(BF16)
    pass_on(2)
    total = stencil(1, total)
    pass_on(3)

    total = stencil(2, total)
    v_of = iota(shape, 0)
    w_of = iota(shape, 1)
    limit = by_sub(counts[0], counts[1], shape)
    inside = (v_of < limit) & (lax.rem(w_of, NV) < limit)
    block = by_sub(total[0:NV], total[NV:ROWS], shape)
    send1[pl.ds(0, NV, stride=8), :] = jnp.where(inside, block, 0.0)

    swap, values = pairing(1 - gx, 0)
    for move in moves[0]:
        move.wait_recv()
    weights = [jnp.where(by_row, values[0][c], values[1][c]) for c in range(3)]
    full = couple(lambda c: near[0, c], lambda c: far[0, c], weights)
    send1[pl.ds(1, NV, stride=8), :] = matched(full, swap)

    _, values = pairing(3 - gy, 1)
    keep_here = keep_last[:, 0:LANES]
    weights = [jnp.where(keep_here, values[1][c], values[0][c]) for c in range(3)]
    for move in moves[1]:
        move.wait_recv()
    twice = lambda ref, c: jnp.concatenate([ref[c], ref[c]], axis=0)
    kept = couple(lambda c: near_y[0, c], lambda c: twice(far_y, c), weights)
    other = couple(lambda c: far_y[c], lambda c: twice(near_y.at[0], c), weights)
    back_out[...] = by_sub(other[0 : NV // 2], other[NV // 2 : NV], (NV // 2, LANES))
    back = pltpu.make_async_remote_copy(
        src_ref=back_out,
        dst_ref=back_in,
        send_sem=back_sem.at[0],
        recv_sem=back_sem.at[1],
        device_id={"gy": 1 - gy},
        device_id_type=MESH,
    )
    back.start()

    swap, values = pairing(4, 2)
    for move in moves[2]:
        move.wait_recv()
    weights = [jnp.where(by_row, values[0][c], values[1][c]) for c in range(3)]
    full = couple(lambda c: near[1, c], lambda c: far[1, c], weights)
    send1[pl.ds(3, NV, stride=8), :] = matched(full, swap)
    weights = [by_sub(values[0][c], values[1][c], (1, LANES)) for c in range(3)]
    full = couple(lambda c: far[1, c], lambda c: near[1, c], weights)
    send1[pl.ds(4, NV, stride=8), :] = matched(full, swap)

    back.wait_recv()
    packed = back_in[...]
    turned = pltpu.roll(packed, NV, 1)
    given = jnp.concatenate(
        [by_sub(packed, turned, packed.shape), by_sub(turned, packed, packed.shape)], axis=0
    )
    send1[pl.ds(2, NV, stride=8), :] = by_sub(
        jnp.where(keep_here, given, kept), jnp.where(keep_here, kept, given), shape
    )

    def exchange(phase, source, target):
        def post(k, carry):
            ring = k >> 3
            step = (ring + 1) >> 1
            ring = 4 + step * (2 * (ring & 1) - 1)
            peer = (((plane + ring) & 7) << 3) + ((gz + k + 1) & 7)
            pltpu.make_async_remote_copy(
                src_ref=source.at[pl.ds(pl.multiple_of(peer * 8, 8), TILE)],
                dst_ref=target.at[pl.ds(pl.multiple_of(gz * 8, 8), TILE)],
                send_sem=a2a_send.at[phase],
                recv_sem=a2a_recv.at[phase],
                device_id={"gz": peer},
                device_id_type=MESH,
            ).start()
            return carry

        lax.fori_loop(0, PEERS - 1, post, 0, unroll=UNROLL_POST)
        mine = pl.ds(pl.multiple_of(gz * 8, 8), 8)
        target[mine, :] = source[mine, :]

    def whole(phase, source, target):
        size = (PEERS - 1) * TILE
        return pltpu.make_async_remote_copy(
            src_ref=source.at[pl.ds(0, size)],
            dst_ref=target.at[pl.ds(0, size)],
            send_sem=a2a_send.at[phase],
            recv_sem=a2a_recv.at[phase],
            device_id={"gz": after},
            device_id_type=MESH,
        )

    pass_on(4)
    exchange(0, send1, recv1)

    line = iota((ROWS, ROWS), 0)
    spot = iota((ROWS, ROWS), 1)
    half = spot // NV
    holder = lax.rem(spot, NV)
    places = owner[...].astype(F32).astype(BF16)
    places = jnp.broadcast_to(places, (8, ROWS))
    want = (2 * lax.rem(line, NV) + line // NV).astype(F32)

    def moved(shift):
        sub = 2 * lax.rem(holder + (PEERS - shift), PEERS) + half
        place = jnp.dot(places, picked(line == sub), preferred_element_type=F32)
        hit = picked(place[0:1, :] == want)
        return jnp.concatenate([hit, hit, hit], axis=1)

    straight, shifted = moved(0), moved(1)
    whole(0, send1, recv1).wait_recv()
    for b in range(5):
        chunk = recv1[pl.ds(b, PEERS, stride=8), :]
        turned = pltpu.roll(chunk, NV, 1)
        chunk = jnp.concatenate(
            [by_sub(chunk, turned, shape), by_sub(turned, chunk, shape)], axis=0
        )
        high = chunk.astype(BF16)
        left = chunk - high.astype(F32)
        middle = left.astype(BF16)
        low = (left - middle.astype(F32)).astype(BF16)
        full = jnp.dot(
            shifted if b == 4 else straight,
            jnp.concatenate([high, middle, low], axis=0),
            preferred_element_type=F32,
        )
        send2[pl.ds(b, PEERS, stride=8), :] = by_sub(full[0:NV], full[NV:ROWS], shape)

    exchange(1, send2, recv2)
    whole(1, send2, recv2).wait_recv()
    out[...] = recv2[...]
    for move in moves[0] + moves[1] + moves[2] + [back, whole(0, send1, recv1), whole(1, send2, recv2)]:
        move.wait_send()


def lay_out(recv2, out):
    gx, gy = lax.axis_index("gx"), lax.axis_index("gy")
    tile = (8, LANES)
    b_of = iota(tile, 0)
    x_at, y_at = 2 - gx, 4 - gy
    plain = (b_of == 0) | ((b_of == x_at) & (gx == 1))
    once = ((b_of == x_at) & (gx == 0)) | ((b_of == y_at) & (gy == 1))
    twice = ((b_of == y_at) & (gy == 0)) | (b_of > 4)
    def place(m, carry):
        pair = [recv2[pl.ds(pl.multiple_of((2 * m + i) * 8, 8), 8), :] for i in range(2)]
        turned = [pltpu.roll(t, NV, 1) for t in pair]
        for p, value in enumerate(
            (by_sub(pair[0], turned[1], tile), by_sub(turned[0], pair[1], tile))
        ):
            value = jnp.where(
                plain,
                value,
                jnp.where(
                    once,
                    pltpu.roll(value, 1, 0),
                    jnp.where(twice, pltpu.roll(value, 2, 0), 0.0),
                ),
            )
            out[:, p, pl.ds(pl.multiple_of(m * LANES, LANES), LANES)] = value[0:7]
        return carry

    lax.fori_loop(0, CELLS // LANES, place, 0, unroll=16)


TILE = 5


def per_device(zvecs, counts, adjacency, mat_id, shear, ratio, owner_map):
    smem = pl.BlockSpec(memory_space=pltpu.SMEM)
    vmem = pl.BlockSpec(memory_space=pltpu.VMEM)
    rows = pl.pallas_call(
        kernel,
        out_shape=pltpu.VMEM((PEERS * 8, LANES), F32),
        in_specs=[pl.BlockSpec(memory_space=pl.ANY), smem, smem, smem, smem, smem, vmem],
        out_specs=vmem,
        scratch_shapes=[
            pltpu.VMEM((3, ROWS, CELLS + 2 * SLAB), BF16),
            pltpu.VMEM((SLAB, 4 * SLAB), BF16),
            pltpu.VMEM((8 * SLAB, 3 * LANES), BF16),
            pltpu.VMEM((3, 3, ROWS, SLAB), BF16),
            pltpu.VMEM((2, 3, ROWS, SLAB), BF16),
            pltpu.VMEM((2, 3, NV, SLAB), BF16),
            pltpu.VMEM((3, NV, SLAB), BF16),
            pltpu.VMEM((NV // 2, LANES), F32),
            pltpu.VMEM((NV // 2, LANES), F32),
            pltpu.VMEM((PEERS * 8, LANES), F32),
            pltpu.VMEM((PEERS * 8, LANES), F32),
            pltpu.VMEM((PEERS * 8, LANES), F32),
            pltpu.VMEM((PEERS * 8, LANES), F32),
            pltpu.SemaphoreType.DMA((3, 2)),
            pltpu.SemaphoreType.DMA((3, 3)),
            pltpu.SemaphoreType.DMA((3, 3)),
            pltpu.SemaphoreType.DMA((2,)),
            pltpu.SemaphoreType.DMA((2,)),
            pltpu.SemaphoreType.DMA((2,)),
            pltpu.SemaphoreType.REGULAR((2,)),
        ],
        compiler_params=pltpu.CompilerParams(collective_id=0, has_side_effects=True),
        name="assemble",
    )(zvecs, counts, adjacency, mat_id, shear, ratio, owner_map)
    rows = pl.pallas_call(
        lay_out,
        out_shape=jax.ShapeDtypeStruct((7, 2, CELLS), F32),
        in_specs=[vmem],
        out_specs=vmem,
        name="lay_out",
    )(pltpu.with_memory_space_constraint(rows, pltpu.VMEM))
    return jnp.transpose(rows, (1, 0, 2))[None]


def solution(mesh):
    placed = (
        P(("gx", "gy", "gz"), None, None, None),
        P(("gx", "gy", "gz")),
        P(("gx", "gy", "gz"), None),
        P(),
        P(),
        P(),
        P(("gx", "gy"), None),
    )
    return jax.shard_map(
        per_device,
        mesh=mesh,
        in_specs=placed,
        out_specs=P(("gx", "gy"), "gz", None, None),
        check_vma=False,
    )
```
